256 devices in a mesh: cells: 128 (over z, y, x_lo, core), lanes: 2 (over x_hi).
Axes of the slice: x: 4 (x_hi: 2, x_lo: 2; x = x_hi * 2 + x_lo), y: 4, z: 8, core: 2. Of those that a mesh axis runs over, the one named last changes fastest.
Arguments:
- centres: float32 [3, 131072], P(None, 'cells'), may hold values from 0 to 4
- seg_lines: float32 [3, 131072], P(None, 'cells'), may hold values from -3 to 3
- burgers: float32 [3, 131072], P(None, 'cells'), may hold values from -6 to 6
- neighbour_blocks: int32 [1024, 16], P('cells', 'lanes'), may hold values from 0 to 39
- seg_nodes: int32 [2, 131072], P(None, 'cells'), may hold values from 0 to 1023
- node_owner: int32 [2, 131072], P(None, 'cells'), may hold values from 0 to 1
- mobility: float32 [131072], P('cells'), may hold values from 0.5 to 4
- cand_target: int32 [4096], P('cells'), may hold values from 0 to 7
- cand_source: int32 [4096], P('cells'), may hold values from 0 to 39
Outputs:
- node_velocity: float32 [3, 131072], P(None, 'cells')
- nearness: float32 [131072], P('cells')
The draws below stay inside these ranges and needn't reach their ends.
All inputs are finite; a program needn't handle non-finite values.
Results may differ from the reference program's by a relative error of at most 0.0003.
Values sent between devices are 32-bit elements; how exact they have to be, the bound alone decides.
A program may use at most 64 MiB of HBM per device.

```python
import math
import jax
import jax.numpy as jnp
from jax import lax

SEG = 1024
BLK = 128
NLIST = 16
NCAND = 32
REACH = 2
NB = 8
WIN = 40
SEGS = 131072
BLOCKS = 1024
CANDS = 4096
N_CELLS = 128


def set_ends(result, stream_key, least, high):
    extent = result.shape
    spot = [jax.random.randint(jax.random.fold_in(stream_key, axis), (), 0, extent[axis]) for axis in range(len(extent))]
    result = result.at[tuple(spot)].set(least)
    longest = extent.index(max(extent))
    spot[longest] = (spot[longest] + 1) % extent[longest]
    return result.at[tuple(spot)].set(high)


def level_of(own_key, dims, split, low, high):
    factor_of = 1.0
    for dim, parts in split:
        steps = jax.random.uniform(jax.random.fold_in(jax.random.fold_in(own_key, 6), dim), (parts,), jnp.float32, low / len(split), high / len(split))
        factor_of = factor_of * jnp.repeat(jnp.exp(steps), dims[dim] // parts).reshape((-1,) + (1,) * (len(dims) - 1 - dim))
    return factor_of


def scatter_about(key, shape, spread, bound, shards=(), kind=jnp.bfloat16):
    gain = level_of(key, shape, shards, -0.22, 0.18) if shards else 1.0
    result = jax.random.normal(key, shape, jnp.float32) * spread * gain
    return jnp.minimum(jnp.maximum(result, -bound), bound).astype(kind)


def setup_inputs(seed: int = 0) -> dict:
    arg_keys = jax.random.split(jax.random.key(seed), 10)
    return {
        "centres": jnp.clip(4.0 * jax.random.uniform(arg_keys[0], (3, SEGS), jnp.float32) ** level_of(arg_keys[0], (3, SEGS), ((1, 128),), -0.2, 0.2), 0.0, 4.0),
        "seg_lines": scatter_about(arg_keys[1], (3, SEGS), 0.5, 3.0, ((1, 128),), jnp.float32),
        "burgers": scatter_about(arg_keys[2], (3, SEGS), 1.0, 6.0, ((1, 128),), jnp.float32),
        "neighbour_blocks": set_ends(jax.random.randint(arg_keys[3], (BLOCKS, NLIST), 0, WIN), jax.random.fold_in(arg_keys[3], 1), 0, WIN - 1).astype(jnp.int32),
        "seg_nodes": set_ends(jax.random.randint(arg_keys[4], (2, SEGS), 0, SEG), jax.random.fold_in(arg_keys[4], 1), 0, SEG - 1).astype(jnp.int32),
        "node_owner": set_ends(jax.random.randint(arg_keys[5], (2, SEGS), 0, 2), jax.random.fold_in(arg_keys[5], 1), 0, 1).astype(jnp.int32),
        "mobility": jnp.clip(jnp.exp(math.log(4.0) - 2.0794415 * jax.random.uniform(arg_keys[6], (SEGS,), jnp.float32) ** level_of(arg_keys[6], (SEGS,), ((0, 128),), -0.2, 0.2)), 0.5, 4.0),
        "cand_target": set_ends(jax.random.randint(arg_keys[7], (CANDS,), 0, NB), jax.random.fold_in(arg_keys[7], 1), 0, NB - 1).astype(jnp.int32),
        "cand_source": set_ends(jax.random.randint(arg_keys[8], (CANDS,), 0, WIN), jax.random.fold_in(arg_keys[8], 1), 0, WIN - 1).astype(jnp.int32),
    }


FORCE_SCALE = 0.02
CORE_SQUARE = 0.25
TIME_STEP = 4.0
HIGH = lax.Precision.HIGHEST

def cross_product(first, second):
    return jnp.stack([first[1] * second[2] - first[2] * second[1], first[2] * second[0] - first[0] * second[2], first[0] * second[1] - first[1] * second[0]])

def tile_forces(own_blocks, source_blocks):
    target_centre = own_blocks[0:3]
    target_line = own_blocks[3:6]
    source_centre = source_blocks[0:3]
    source_line = source_blocks[3:6]
    source_burgers = source_blocks[6:9]
    along = jnp.einsum('ckj,cki->kij', source_burgers, target_line, precision=HIGH)
    separation = target_centre[:, :, :, None] - source_centre[:, :, None, :]
    square = lax.optimization_barrier(jnp.sum(separation * separation, axis=0)) + CORE_SQUARE
    inverse = lax.rsqrt(square)
    weight = along * inverse * inverse * inverse
    summed_line = jnp.einsum('kij,ckj->cki', weight, source_line, precision=HIGH)
    summed_moment = jnp.einsum('kij,ckj->cki', weight, cross_product(source_line, source_centre), precision=HIGH)
    return FORCE_SCALE * (cross_product(summed_line, target_centre) - summed_moment)

def block_forces(own_blocks, window_blocks, block_lists):

    def add_entry(summed, column):
        chosen = jnp.take(window_blocks, column, axis=1)
        return (summed + tile_forces(own_blocks, chosen), None)
    initial = jnp.zeros((3,) + own_blocks.shape[1:], jnp.float32)
    summed, unused = lax.scan(add_entry, initial, jnp.transpose(block_lists))
    return summed

def swept_tiles(own_blocks, window_blocks, targets, sources):
    target_side = jnp.take(own_blocks, targets, axis=1)
    source_side = jnp.take(window_blocks, sources, axis=1)
    separation = target_side[0:3, :, :, None] - source_side[0:3, :, None, :]
    motion = TIME_STEP * (target_side[3:6, :, :, None] - source_side[3:6, :, None, :])
    approach = lax.optimization_barrier(jnp.sum(separation * motion, axis=0))
    motion_square = lax.optimization_barrier(jnp.sum(motion * motion, axis=0))
    fraction = jnp.clip(-approach / (motion_square + CORE_SQUARE), 0.0, 1.0)
    closest = separation + fraction[None] * motion
    distance = lax.optimization_barrier(jnp.sum(closest * closest, axis=0))
    summed = lax.optimization_barrier(jnp.sum(jnp.exp(-distance), axis=2))
    selector = (targets[:, None] == jnp.arange(own_blocks.shape[1], dtype=jnp.int32)[None, :]).astype(jnp.float32)
    return jnp.einsum('nk,nb->kb', selector, summed, precision=HIGH)

def deposit(deposits, node_ids, keep_mask, node_count):
    masked = deposits * keep_mask.astype(jnp.float32)[None, :]
    return jnp.transpose(jax.ops.segment_sum(jnp.transpose(masked), node_ids, num_segments=node_count))

def end_velocity(velocity, next_velocity, node_ids, owner_map):
    return jnp.where(owner_map[None, :] == 0, jnp.take(velocity, node_ids, axis=1), jnp.take(next_velocity, node_ids, axis=1))

def window_of(fields, domain):
    picks = [lax.dynamic_index_in_dim(fields, (domain + offset) % N_CELLS, 1, keepdims=False) for offset in range(-REACH, REACH + 1)]
    return jnp.concatenate(picks, axis=1)

def reference(centres, seg_lines, burgers, neighbour_blocks, seg_nodes, node_owner, mobility, cand_target, cand_source):
    domains = jnp.arange(N_CELLS, dtype=jnp.int32)
    fields = jnp.concatenate([centres, seg_lines, burgers], 0).reshape(9, N_CELLS, SEG)
    block_lists = neighbour_blocks.reshape(N_CELLS, NB, NLIST)

    def forces_of(domain):
        own_blocks = lax.dynamic_index_in_dim(fields, domain, 1, keepdims=False).reshape(9, NB, BLK)
        window_blocks = window_of(fields, domain).reshape(9, WIN, BLK)
        chosen_lists = lax.dynamic_index_in_dim(block_lists, domain, 0, keepdims=False)
        return block_forces(own_blocks, window_blocks, chosen_lists).reshape(3, SEG)
    forces = lax.map(forces_of, domains)
    lengths = jnp.sqrt(lax.optimization_barrier(jnp.sum(seg_lines * seg_lines, axis=0))).reshape(N_CELLS, SEG)
    deposits = jnp.concatenate([0.5 * forces, 0.5 * lengths[:, None, :]], axis=1)
    node_ids = seg_nodes.reshape(2, N_CELLS, SEG)
    owner_map = node_owner.reshape(2, N_CELLS, SEG)

    def split_parts(domain_deposits, first_ids, second_ids, first_owner, second_owner):
        own_part = deposit(domain_deposits, first_ids, first_owner == 0, SEG) + deposit(domain_deposits, second_ids, second_owner == 0, SEG)
        next_part = deposit(domain_deposits, first_ids, first_owner == 1, SEG) + deposit(domain_deposits, second_ids, second_owner == 1, SEG)
        return (own_part, next_part)
    own_part, next_part = jax.vmap(split_parts)(deposits, node_ids[0], node_ids[1], owner_map[0], owner_map[1])
    totals = own_part + jnp.roll(next_part, 1, axis=0)
    velocity = mobility.reshape(N_CELLS, 1, SEG) * totals[:, 0:3] / (1.0 + totals[:, 3:4])
    next_velocity = jnp.roll(velocity, -1, axis=0)
    seg_velocity = 0.5 * (jax.vmap(end_velocity)(velocity, next_velocity, node_ids[0], owner_map[0]) + jax.vmap(end_velocity)(velocity, next_velocity, node_ids[1], owner_map[1]))
    motion_fields = jnp.concatenate([centres.reshape(3, N_CELLS, SEG), jnp.transpose(seg_velocity, (1, 0, 2))], axis=0)
    targets = cand_target.reshape(N_CELLS, NCAND)
    sources = cand_source.reshape(N_CELLS, NCAND)

    def nearness_of(domain):
        own_blocks = lax.dynamic_index_in_dim(motion_fields, domain, 1, keepdims=False).reshape(6, NB, BLK)
        window_blocks = window_of(motion_fields, domain).reshape(6, WIN, BLK)
        return swept_tiles(own_blocks, window_blocks, lax.dynamic_index_in_dim(targets, domain, 0, keepdims=False), lax.dynamic_index_in_dim(sources, domain, 0, keepdims=False)).reshape(SEG)
    nearness = lax.map(nearness_of, domains)
    return (jnp.transpose(velocity, (1, 0, 2)).reshape(3, N_CELLS * SEG), nearness.reshape(N_CELLS * SEG))
```

```python
import functools

import jax
import jax.numpy as jnp
from jax import lax
from jax.experimental import pallas as pl
from jax.experimental.pallas import tpu as pltpu
from jax.sharding import PartitionSpec as P

BLK = 128
NB = 8
SEG = BLK * NB
HALF = NB // 2
NENT = 8
NCAND = 32
WIDE = 2
FAR = 3
SPAN = 2 * FAR + 1
FORCE_SCALE = 0.02
CORE_SQUARE = 0.25
TIME_STEP = 4.0
CENTRE = 2.0
F32 = jnp.float32
BF16 = jnp.bfloat16
MESH = pl.DeviceIdType.MESH
NT = (((1,), (1,)), ((), ()))
NN = (((1,), (0,)), ((), ()))


def rounded(x):
    return x.astype(BF16).astype(F32)


def two_parts(x):
    top = rounded(x)
    return top, rounded(x - top)


def three_parts(x):
    top = rounded(x)
    rest = x - top
    mid = rounded(rest)
    return top, mid, rounded(rest - mid)


def kernel(
    n_cells,
    lists_hbm,
    cand_t,
    cand_s,
    centres_hbm,
    lines_hbm,
    burgers_hbm,
    nodes_hbm,
    owner_hbm,
    mobility,
    velocity_out,
    nearness_out,
    win_c,
    win_l,
    win_b,
    codes_n,
    codes_o,
    list_own,
    list_far_v,
    list_far,
    feat,
    tall,
    feat_q,
    feat_a,
    pull,
    tgt_q,
    tgt_a,
    onehot,
    mask16,
    drag_send,
    drag_recv,
    eff,
    fbuf,
    vel,
    mot,
    local_sem,
    send_a,
    recv_a,
    send_n,
    recv_n,
    misc_sem,
    send_b,
    recv_b,
):
    me = lax.axis_index("cells")
    lane = lax.axis_index("lanes")
    other = 1 - lane

    def cell(offset):
        return lax.rem(me + (offset + n_cells), n_cells)

    partners = [
        (o, far) for o in (0, 1, -1, 2, -2, 3, -3) for far in (False, True) if (o, far) != (0, False)
    ]

    barrier = pltpu.get_barrier_semaphore()
    for o, far in partners:
        pl.semaphore_signal(
            barrier, inc=1, device_id=(cell(o), other if far else lane), device_id_type=MESH
        )
    own_copies = [
        pltpu.make_async_copy(centres_hbm, win_c.at[WIDE], local_sem.at[0]),
        pltpu.make_async_copy(lines_hbm, win_l.at[WIDE], local_sem.at[1]),
        pltpu.make_async_copy(burgers_hbm, win_b.at[WIDE], local_sem.at[2]),
        pltpu.make_async_copy(nodes_hbm, codes_n.at[FAR], local_sem.at[3]),
        pltpu.make_async_copy(owner_hbm, codes_o.at[FAR], local_sem.at[4]),
        pltpu.make_async_copy(lists_hbm, list_own, local_sem.at[5]),
    ]
    for copy in own_copies:
        copy.start()
    pl.semaphore_wait(barrier, len(partners))

    def remote(src, dst, send, recv, o, far):
        return pltpu.make_async_remote_copy(
            src_ref=src,
            dst_ref=dst,
            send_sem=send,
            recv_sem=recv,
            device_id=(cell(o), other if far else lane),
            device_id_type=MESH,
        )

    sends_a = {}
    for o in (1, -1, 2, -2):
        for a, (src, dst) in enumerate(
            ((centres_hbm, win_c), (lines_hbm, win_l), (burgers_hbm, win_b))
        ):
            slot = WIDE - o
            sends_a[(o, a)] = remote(
                src, dst.at[slot], send_a.at[WIDE + o, a], recv_a.at[slot, a], o, False
            )
            sends_a[(o, a)].start()
    list_copy = remote(lists_hbm, list_far_v, misc_sem.at[0], misc_sem.at[1], 0, True)
    list_copy.start()
    sends_n = {}
    for o in (1, -1, 2, -2, 3, -3):
        for a, (src, dst) in enumerate(((nodes_hbm, codes_n), (owner_hbm, codes_o))):
            slot = FAR - o
            sends_n[(o, a)] = remote(
                src, dst.at[slot], send_n.at[FAR + o, a], recv_n.at[slot, a], o, False
            )
            sends_n[(o, a)].start()
    for copy in own_copies:
        copy.wait()

    def build_codes(slot):
        for e in range(2):
            node = codes_n[slot, e : e + 1, :] + SEG * codes_o[slot, e : e + 1, :]
            low = jnp.bitwise_and(node, BLK - 1)
            high = lax.shift_right_logical(node, 7)
            span = pl.ds(e * SEG, SEG)
            rows = lax.broadcasted_iota(jnp.int32, (BLK, SEG), 0)
            onehot[slot, :, span] = (rows == low).astype(F32).astype(BF16)
            rows16 = lax.broadcasted_iota(jnp.int32, (16, SEG), 0)
            mask16[slot, :, span] = (rows16 == high).astype(F32)

    feat[...] = jnp.zeros_like(feat)

    def build_source(s):
        c = win_c[s] - CENTRE
        ch, cm, cl = three_parts(c)
        for g, part in enumerate((ch, cm, ch, cm, cl, ch)):
            feat[8 * g : 8 * g + 3, :] = part
        rows = [win_c[s, k : k + 1, :] - CENTRE for k in range(3)]
        square = rows[0] * rows[0] + rows[1] * rows[1] + rows[2] * rows[2] + CORE_SQUARE
        for k, part in enumerate(three_parts(square)):
            feat[48 + k : 49 + k, :] = part
            feat[51 + k : 52 + k, :] = jnp.ones_like(part)
        bh, bm, bl = three_parts(win_b[s])
        for g, part in enumerate((bh, bm, bh, bm, bl, bh)):
            feat[64 + 8 * g : 64 + 8 * g + 3, :] = part
        line = [win_l[s, k : k + 1, :] for k in range(3)]
        moment = (
            line[1] * rows[2] - line[2] * rows[1],
            line[2] * rows[0] - line[0] * rows[2],
            line[0] * rows[1] - line[1] * rows[0],
        )
        for k in range(3):
            lh, ll = two_parts(line[k])
            mh, ml = two_parts(moment[k])
            for g, part in enumerate((lh, mh, ll, ml)):
                tall[8 * g + k : 8 * g + k + 1, :] = part
        for b in range(NB):
            cut = slice(b * BLK, (b + 1) * BLK)
            feat_q[s * NB + b] = feat[0:64, cut].astype(BF16)
            feat_a[s * NB + b] = feat[64:128, cut].astype(BF16)
            pull[s * NB + b] = tall[:, cut].astype(BF16)
            mot[s * NB + b, 0:3, :] = win_c[s, :, cut]

    tall[...] = jnp.zeros_like(tall)
    build_source(WIDE)

    c = win_c[WIDE] - CENTRE
    ch, cm, cl = three_parts(c)
    for g, part in enumerate((ch, ch, cm, cm, ch, cl)):
        feat[8 * g : 8 * g + 3, :] = -2.0 * part
    rows = [win_c[WIDE, k : k + 1, :] - CENTRE for k in range(3)]
    square = rows[0] * rows[0] + rows[1] * rows[1] + rows[2] * rows[2]
    for k, part in enumerate(three_parts(square)):
        feat[51 + k : 52 + k, :] = part
        feat[48 + k : 49 + k, :] = jnp.ones_like(part)
    lh, lm, ll = three_parts(win_l[WIDE])
    for g, part in enumerate((lh, lh, lm, lm, lh, ll)):
        feat[64 + 8 * g : 64 + 8 * g + 3, :] = part
    for b in range(NB):
        cut = slice(b * BLK, (b + 1) * BLK)
        turned = jnp.transpose(feat[:, cut])
        tgt_q[b] = turned[:, 0:64].astype(BF16)
        tgt_a[b] = turned[:, 64:128].astype(BF16)

    build_codes(FAR)
    line = [win_l[WIDE, k : k + 1, :] for k in range(3)]
    length = 0.5 * jnp.sqrt(line[0] * line[0] + line[1] * line[1] + line[2] * line[2])
    drag = jnp.zeros((32, BLK), F32)
    for e in range(2):
        span = slice(e * SEG, (e + 1) * SEG)
        mask = mask16[FAR, :, span] > 0.5
        parts = [
            jnp.where(mask, jnp.broadcast_to(part, (16, SEG)), 0.0) for part in two_parts(length)
        ]
        drag = drag + lax.dot_general(
            jnp.concatenate(parts, axis=0).astype(BF16),
            onehot[FAR, :, span],
            NT,
            preferred_element_type=F32,
        )
    drag_send[...] = drag[8:16] + drag[24:32]
    drag_copy = remote(drag_send, drag_recv, misc_sem.at[2], misc_sem.at[3], 1, False)
    drag_copy.start()
    own_drag = drag[0:8] + drag[16:24]

    for o in (1, -1, 2, -2):
        for a in range(3):
            sends_a[(-o, a)].wait_recv()
        build_source(WIDE + o)
    list_copy.wait_recv()
    to_smem = pltpu.make_async_copy(list_far_v, list_far, misc_sem.at[4])
    to_smem.start()
    to_smem.wait()
    drag_copy.wait_recv()
    eff_all = mobility[...] / (1.0 + (own_drag + drag_recv[...]))
    for b in range(NB):
        eff[b] = eff_all[b : b + 1, :]

    def one_target(t, carry):
        block = HALF * lane + t
        left_q = tgt_q[block]
        left_a = tgt_a[block]
        total = jnp.zeros((32, BLK), F32)
        for lists in (list_own, list_far):
            for e in range(NENT):
                source = lists[block, e]
                q = lax.dot_general(left_q, feat_q[source], NN, preferred_element_type=F32)
                along = lax.dot_general(left_a, feat_a[source], NN, preferred_element_type=F32)
                inverse = lax.rsqrt(q)
                weight = along * inverse * inverse * inverse
                top = weight.astype(BF16)
                low = (weight - top.astype(F32)).astype(BF16)
                pulls = pull[source]
                total = total + lax.dot_general(pulls, top, NT, preferred_element_type=F32)
                total = total + lax.dot_general(pulls, low, NT, preferred_element_type=F32)
        total = total[0:16] + total[16:32]
        cut = pl.ds(pl.multiple_of(block * BLK, BLK), BLK)
        x, y, z = (win_c[WIDE, k : k + 1, cut] - CENTRE for k in range(3))
        sx, sy, sz = (total[k : k + 1] for k in range(3))
        scale = 0.5 * FORCE_SCALE
        fbuf[FAR, block, 0:1, :] = scale * (sy * z - sz * y - total[8:9])
        fbuf[FAR, block, 1:2, :] = scale * (sz * x - sx * z - total[9:10])
        fbuf[FAR, block, 2:3, :] = scale * (sx * y - sy * x - total[10:11])
        fbuf[FAR, block, 3:4, :] = eff[block]
        return carry

    lax.fori_loop(0, HALF, one_target, 0)

    mine = pl.ds(HALF * lane, HALF)
    sends_b = []
    for o, far in partners:
        slot = FAR - o
        copy = remote(
            fbuf.at[FAR, mine],
            fbuf.at[slot, mine],
            send_b.at[FAR + o, int(far)],
            recv_b.at[slot, int(far)],
            o,
            far,
        )
        copy.start()
        sends_b.append(copy)

    for o in (1, -1, 2, -2, 3, -3):
        for a in range(2):
            sends_n[(-o, a)].wait_recv()
        build_codes(FAR + o)

    own_part = {}
    next_part = {}
    recv_of = {(o, far): copy for (o, far), copy in zip(partners, sends_b)}
    for o in (0, 1, -1, 2, -2, 3, -3):
        slot = FAR + o
        for far in (False, True):
            if (-o, far) in recv_of:
                recv_of[(-o, far)].wait_recv()
        forces = jnp.concatenate([fbuf[slot, b] for b in range(NB)], axis=1)
        parts = two_parts(forces)
        total = jnp.zeros((96, BLK), F32)
        for e in range(2):
            span = slice(e * SEG, (e + 1) * SEG)
            mask = mask16[slot, :, span] > 0.5
            stack = [
                jnp.where(mask, jnp.broadcast_to(part[k : k + 1], (16, SEG)), 0.0)
                for part in parts
                for k in range(3)
            ]
            total = total + lax.dot_general(
                jnp.concatenate(stack, axis=0).astype(BF16),
                onehot[slot, :, span],
                NT,
                preferred_element_type=F32,
            )
        total = total[0:48] + total[48:96]
        own_part[o] = [total[16 * k : 16 * k + 8] for k in range(3)]
        next_part[o] = [total[16 * k + 8 : 16 * k + 16] for k in range(3)]

    for o in range(-WIDE, FAR + 1):
        eff_o = jnp.concatenate([fbuf[FAR + o, b, 3:4, :] for b in range(NB)], axis=0)
        for k in range(3):
            value = eff_o * (own_part[o][k] + next_part[o - 1][k])
            vel[FAR + o, k] = value
            if o == 0:
                for b in range(NB):
                    velocity_out[k : k + 1, b * BLK : (b + 1) * BLK] = value[b : b + 1, :]

    for o in range(-WIDE, WIDE + 1):
        slot = FAR + o
        table = jnp.concatenate(
            [piece for k in range(3) for piece in (vel[slot, k], vel[slot + 1, k])], axis=0
        )
        stack = jnp.concatenate(two_parts(table), axis=0).astype(BF16)
        both = None
        for e in range(2):
            span = slice(e * SEG, (e + 1) * SEG)
            picked = lax.dot_general(stack, onehot[slot, :, span], NN, preferred_element_type=F32)
            picked = picked[0:48] + picked[48:96]
            mask = mask16[slot, :, span] > 0.5
            kept = [jnp.where(mask, picked[16 * k : 16 * k + 16], 0.0) for k in range(3)]
            both = kept if both is None else [x + y for x, y in zip(both, kept)]
        for k in range(3):
            row = 0.5 * TIME_STEP * jnp.sum(both[k], axis=0, keepdims=True)
            for b in range(NB):
                mot[(WIDE + o) * NB + b, 3 + k : 4 + k, :] = row[:, b * BLK : (b + 1) * BLK]

    block_rows = lax.broadcasted_iota(jnp.int32, (NB, BLK), 0)

    def one_pair(n, near):
        target = cand_t[n]
        source = cand_s[n]
        here = mot[WIDE * NB + target]
        there = jnp.transpose(mot[source])
        goal = [jnp.broadcast_to(here[k : k + 1], (8, BLK)) for k in range(6)]
        total = jnp.zeros((8, BLK), F32)
        for r in range(BLK // 8):
            chunk = there[8 * r : 8 * r + 8]
            gap = [goal[k] - jnp.broadcast_to(chunk[:, k : k + 1], (8, BLK)) for k in range(6)]
            x, y, z, u, v, w = gap
            approach = x * u + y * v + z * w
            square = u * u + v * v + w * w
            fraction = jnp.clip(-approach / (square + CORE_SQUARE), 0.0, 1.0)
            x = x + fraction * u
            y = y + fraction * v
            z = z + fraction * w
            total = total + jnp.exp(-(x * x + y * y + z * z))
        row = jnp.sum(total, axis=0, keepdims=True)
        return near + jnp.where(block_rows == target, jnp.broadcast_to(row, (NB, BLK)), 0.0)

    nearness_out[...] = lax.fori_loop(0, NCAND, one_pair, jnp.zeros((NB, BLK), F32))

    for copy in list(sends_a.values()) + list(sends_n.values()) + sends_b + [list_copy, drag_copy]:
        copy.wait_send()


def local(
    centres,
    seg_lines,
    burgers,
    neighbour_blocks,
    seg_nodes,
    node_owner,
    mobility,
    cand_target,
    cand_source,
):
    n_cells = lax.axis_size("cells")
    window = 2 * WIDE + 1
    anywhere = pl.BlockSpec(memory_space=pl.ANY)
    vmem = pl.BlockSpec(memory_space=pltpu.VMEM)
    smem = pl.BlockSpec(memory_space=pltpu.SMEM)
    velocity, nearness = pl.pallas_call(
        functools.partial(kernel, n_cells),
        name="dislocation_step",
        out_shape=(
            jax.ShapeDtypeStruct((3, SEG), F32),
            jax.ShapeDtypeStruct((NB, BLK), F32),
        ),
        in_specs=[anywhere, smem, smem] + [anywhere] * 5 + [vmem],
        out_specs=(vmem, vmem),
        scratch_shapes=[
            pltpu.VMEM((window, 3, SEG), F32),
            pltpu.VMEM((window, 3, SEG), F32),
            pltpu.VMEM((window, 3, SEG), F32),
            pltpu.VMEM((SPAN, 2, SEG), jnp.int32),
            pltpu.VMEM((SPAN, 2, SEG), jnp.int32),
            pltpu.SMEM((NB, NENT), jnp.int32),
            pltpu.VMEM((NB, NENT), jnp.int32),
            pltpu.SMEM((NB, NENT), jnp.int32),
            pltpu.VMEM((128, SEG), F32),
            pltpu.VMEM((32, SEG), F32),
            pltpu.VMEM((window * NB, 64, BLK), BF16),
            pltpu.VMEM((window * NB, 64, BLK), BF16),
            pltpu.VMEM((window * NB, 32, BLK), BF16),
            pltpu.VMEM((NB, BLK, 64), BF16),
            pltpu.VMEM((NB, BLK, 64), BF16),
            pltpu.VMEM((SPAN, BLK, 2 * SEG), BF16),
            pltpu.VMEM((SPAN, 16, 2 * SEG), F32),
            pltpu.VMEM((NB, BLK), F32),
            pltpu.VMEM((NB, BLK), F32),
            pltpu.VMEM((NB, 1, BLK), F32),
            pltpu.VMEM((SPAN, NB, 4, BLK), F32),
            pltpu.VMEM((SPAN, 3, NB, BLK), F32),
            pltpu.VMEM((window * NB, 8, BLK), F32),
            pltpu.SemaphoreType.DMA((6,)),
            pltpu.SemaphoreType.DMA((window, 3)),
            pltpu.SemaphoreType.DMA((window, 3)),
            pltpu.SemaphoreType.DMA((SPAN, 2)),
            pltpu.SemaphoreType.DMA((SPAN, 2)),
            pltpu.SemaphoreType.DMA((5,)),
            pltpu.SemaphoreType.DMA((SPAN, 2)),
            pltpu.SemaphoreType.DMA((SPAN, 2)),
        ],
        compiler_params=pltpu.CompilerParams(
            collective_id=0, has_side_effects=True, vmem_limit_bytes=40 * 2**20
        ),
    )(
        neighbour_blocks,
        cand_target,
        cand_source,
        centres,
        seg_lines,
        burgers,
        seg_nodes,
        node_owner,
        mobility.reshape(NB, BLK),
    )
    return velocity, nearness.reshape(SEG)


def solution(mesh):
    in_specs = (
        P(None, "cells"),
        P(None, "cells"),
        P(None, "cells"),
        P("cells", "lanes"),
        P(None, "cells"),
        P(None, "cells"),
        P("cells"),
        P("cells"),
        P("cells"),
    )
    out_specs = (P(None, "cells"), P("cells"))
    return jax.shard_map(local, mesh=mesh, in_specs=in_specs, out_specs=out_specs, check_vma=False)
```

```python
import functools
import math

import jax
import jax.numpy as jnp
from jax import lax
from jax.experimental import pallas as pl
from jax.experimental.pallas import tpu as pltpu
from jax.sharding import PartitionSpec as P

BLK = 128
NB = 8
SEG = BLK * NB
HALF = NB // 2
NENT = 8
NCAND = 32
WIDE = 2
FAR = 3
SPAN = 2 * FAR + 1
WAITS = {0: (0, 1, -1), 2: (2, -2, 3, -3)}
FORCE_SCALE = 0.02
CORE_SQUARE = 0.25
TIME_STEP = 4.0
CENTRE = 2.0
TOGETHER = 8
F32 = jnp.float32
BF16 = jnp.bfloat16
MESH = pl.DeviceIdType.MESH
NT = (((1,), (1,)), ((), ()))
NN = (((1,), (0,)), ((), ()))


def rounded(x):
    return x.astype(BF16).astype(F32)


def two_parts(x):
    top = rounded(x)
    return top, rounded(x - top)


def three_parts(x):
    top = rounded(x)
    rest = x - top
    mid = rounded(rest)
    return top, mid, rounded(rest - mid)


def kernel(
    n_cells,
    lists_hbm,
    cand_t,
    cand_s,
    centres_hbm,
    lines_hbm,
    burgers_hbm,
    nodes_hbm,
    owner_hbm,
    mobility,
    velocity_out,
    nearness_out,
    win_c,
    win_l,
    win_b,
    codes_n,
    codes_o,
    list_own,
    list_far_v,
    list_far,
    dense,
    stage_f,
    stage_p,
    stage_q,
    stage_a,
    stage_n,
    stage_t,
    feat,
    pull,
    target,
    goal,
    codes_d,
    onehot,
    mask16,
    drag_send,
    drag_recv,
    eff,
    fbuf,
    vel,
    local_sem,
    send_a,
    recv_a,
    send_n,
    recv_n,
    misc_sem,
    send_b,
    recv_b,
):
    me = lax.axis_index("cells")
    lane = lax.axis_index("lanes")
    other = 1 - lane

    def cell(offset):
        return lax.rem(me + (offset + n_cells), n_cells)

    partners = [
        (o, far) for o in (0, 1, -1, 2, -2, 3, -3) for far in (False, True) if (o, far) != (0, False)
    ]

    barrier = pltpu.get_barrier_semaphore()
    for o, far in partners:
        pl.semaphore_signal(
            barrier, inc=1, device_id=(cell(o), other if far else lane), device_id_type=MESH
        )
    own_copies = [
        pltpu.make_async_copy(centres_hbm, win_c.at[WIDE], local_sem.at[0]),
        pltpu.make_async_copy(lines_hbm, win_l.at[WIDE], local_sem.at[1]),
        pltpu.make_async_copy(burgers_hbm, win_b.at[WIDE], local_sem.at[2]),
        pltpu.make_async_copy(nodes_hbm, codes_n.at[FAR], local_sem.at[3]),
        pltpu.make_async_copy(owner_hbm, codes_o.at[FAR], local_sem.at[4]),
        pltpu.make_async_copy(lists_hbm, list_own, local_sem.at[5]),
    ]
    for copy in own_copies:
        copy.start()
    pl.semaphore_wait(barrier, len(partners))

    def remote(src, dst, send, recv, o, far):
        return pltpu.make_async_remote_copy(
            src_ref=src,
            dst_ref=dst,
            send_sem=send,
            recv_sem=recv,
            device_id=(cell(o), other if far else lane),
            device_id_type=MESH,
        )

    sends_a = {}
    for o in (1, -1, 2, -2):
        for a, (src, dst) in enumerate(
            ((centres_hbm, win_c), (lines_hbm, win_l), (burgers_hbm, win_b))
        ):
            slot = WIDE - o
            sends_a[(o, a)] = remote(
                src, dst.at[slot], send_a.at[WIDE + o, a], recv_a.at[slot, a], o, False
            )
            sends_a[(o, a)].start()
    list_copy = remote(lists_hbm, list_far_v, misc_sem.at[0], misc_sem.at[1], 0, True)
    list_copy.start()
    sends_n = {}
    for o in (1, -1, 2, -2, 3, -3):
        for a, (src, dst) in enumerate(((nodes_hbm, codes_n), (owner_hbm, codes_o))):
            slot = FAR - o
            sends_n[(o, a)] = remote(
                src, dst.at[slot], send_n.at[FAR + o, a], recv_n.at[slot, a], o, False
            )
            sends_n[(o, a)].start()
    for copy in own_copies:
        copy.wait()

    def build_codes(slot):
        for e in range(2):
            node = codes_n[slot, e : e + 1, :] + SEG * codes_o[slot, e : e + 1, :]
            low = jnp.bitwise_and(node, BLK - 1)
            high = lax.shift_right_logical(node, 7)
            span = pl.ds(e * SEG, SEG)
            rows = lax.broadcasted_iota(jnp.int32, (BLK, SEG), 0)
            onehot[slot, :, span] = (rows == low).astype(F32).astype(BF16)
            rows16 = lax.broadcasted_iota(jnp.int32, (16, SEG), 0)
            mask16[slot, :, span] = (rows16 == high).astype(F32)
            for b in range(NB):
                codes_d[slot, e, b : b + 1, :] = node[:, b * BLK : (b + 1) * BLK]

    ones = jnp.ones((NB, BLK), F32)
    zeros = jnp.zeros((NB, BLK), F32)

    def odd(rows):
        return len(rows) | 1

    def put(ref, base, rows):
        for r, row in enumerate(rows):
            ref[pl.ds(base * odd(rows) + r, NB, stride=odd(rows)), :] = row

    def dense_fields(s):
        for a, win in enumerate((win_c, win_l, win_b)):
            for b in range(NB):
                dense[s, pl.ds(24 * a + b, 3, stride=NB), :] = win[s, :, b * BLK : (b + 1) * BLK]
        parts = [dense[s, NB * k : NB * (k + 1), :] for k in range(9)]
        return [x - CENTRE for x in parts[0:3]], parts[3:6], parts[6:9]

    def dot3(x, y):
        return x[0] * y[0] + x[1] * y[1] + x[2] * y[2]

    def split3(rows):
        return [list(x) for x in zip(*(three_parts(row) for row in rows))]

    def split2(rows):
        return [list(x) for x in zip(*(two_parts(row) for row in rows))]

    def build_source(s):
        c, line, burg = dense_fields(s)
        ch, cm, cl = split3(c)
        sh, sm, sl = three_parts(dot3(c, c) + CORE_SQUARE)
        bh, bm = split2(burg)
        rows = ch + cm + [sh, sm] + ch + cm + [ones, ones] + cl + ch + [sl, ones]
        rows += (bh + bm + [zeros, zeros]) * 2 + [zeros] * 8
        put(stage_f, s * NB, rows)
        moment = [
            line[1] * c[2] - line[2] * c[1],
            line[2] * c[0] - line[0] * c[2],
            line[0] * c[1] - line[1] * c[0],
        ]
        high, low = split2(line + moment)
        put(stage_p, s * NB, high + [zeros, zeros] + low + [zeros, zeros])
        for b in range(s * NB, (s + 1) * NB):
            feat[b] = stage_f[49 * b : 49 * b + 48, :].astype(BF16)
            pull[b] = stage_p[17 * b : 17 * b + 16, :].astype(BF16)
        return c, line, (ch, cm, cl), (sh, sm)

    centre_own, line_own, (ch, cm, cl), own_square = build_source(WIDE)

    def twice(rows):
        return [-2.0 * row for row in rows]

    zh, zm, zl = three_parts(dot3(centre_own, centre_own))
    lh, lm = split2(line_own)
    rows = twice(ch) * 2 + [ones, ones] + twice(cm) * 2 + [zh, zm]
    rows += twice(ch) + twice(cl) + [ones, zl]
    put(stage_q, 0, rows)
    put(stage_a, 0, lh * 2 + [zeros, zeros] + lm * 2 + [zeros, zeros])
    for b in range(NB):
        left = jnp.concatenate([stage_q[25 * b : 25 * b + 24, :], jnp.zeros((24, BLK), F32)], 0)
        target[b, 0:BLK, :] = jnp.transpose(left).astype(BF16)
        left = jnp.concatenate(
            [
                jnp.zeros((24, BLK), F32),
                stage_a[17 * b : 17 * b + 16, :],
                jnp.zeros((8, BLK), F32),
            ],
            0,
        )
        target[b, BLK : 2 * BLK, :] = jnp.transpose(left).astype(BF16)

    build_codes(FAR)
    line = [win_l[WIDE, k : k + 1, :] for k in range(3)]
    length = 0.5 * jnp.sqrt(dot3(line, line))
    drag = jnp.zeros((32, BLK), F32)
    for e in range(2):
        span = slice(e * SEG, (e + 1) * SEG)
        mask = mask16[FAR, :, span] > 0.5
        parts = [
            jnp.where(mask, jnp.broadcast_to(part, (16, SEG)), 0.0) for part in two_parts(length)
        ]
        drag = drag + lax.dot_general(
            jnp.concatenate(parts, axis=0).astype(BF16),
            onehot[FAR, :, span],
            NT,
            preferred_element_type=F32,
        )
    drag_send[...] = drag[8:16] + drag[24:32]
    drag_copy = remote(drag_send, drag_recv, misc_sem.at[2], misc_sem.at[3], 1, False)
    drag_copy.start()
    own_drag = drag[0:8] + drag[16:24]

    kept_centres = {0: (centre_own, line_own, (ch, cm, cl), own_square)}
    for o in (1, -1, 2, -2):
        for a in range(3):
            sends_a[(-o, a)].wait_recv()
        kept_centres[o] = build_source(WIDE + o)
    list_copy.wait_recv()
    to_smem = pltpu.make_async_copy(list_far_v, list_far, misc_sem.at[4])
    to_smem.start()
    to_smem.wait()
    drag_copy.wait_recv()
    eff_all = mobility[...] / (1.0 + (own_drag + drag_recv[...]))
    for b in range(NB):
        eff[b] = eff_all[b : b + 1, :]

    def one_target(t, carry):
        block = HALF * lane + t
        left = target[block]
        total = jnp.zeros((16, BLK), F32)
        for lists in (list_own, list_far):
            for e in range(0, NENT, 2):
                first = lists[block, e]
                second = lists[block, e + 1]
                right = jnp.concatenate([feat[first], feat[second]], axis=1)
                both = lax.dot_general(left, right, NN, preferred_element_type=F32)
                inverse = lax.rsqrt(both[0:BLK])
                weight = both[BLK : 2 * BLK] * inverse * inverse * inverse
                top = weight.astype(BF16)
                low = (weight - top.astype(F32)).astype(BF16)
                pulls = jnp.concatenate([pull[first], pull[second]], axis=1)
                total = total + lax.dot_general(pulls, top, NT, preferred_element_type=F32)
                total = total + lax.dot_general(pulls, low, NT, preferred_element_type=F32)
        total = total[0:8] + total[8:16]
        cut = pl.ds(pl.multiple_of(block * BLK, BLK), BLK)
        x, y, z = (win_c[WIDE, k : k + 1, cut] - CENTRE for k in range(3))
        sx, sy, sz = (total[k : k + 1] for k in range(3))
        scale = 0.5 * FORCE_SCALE
        fbuf[FAR, block, 0:1, :] = scale * (sy * z - sz * y - total[3:4])
        fbuf[FAR, block, 1:2, :] = scale * (sz * x - sx * z - total[4:5])
        fbuf[FAR, block, 2:3, :] = scale * (sx * y - sy * x - total[5:6])
        fbuf[FAR, block, 3:4, :] = eff[block]
        return carry

    lax.fori_loop(0, HALF, one_target, 0)

    mine = pl.ds(HALF * lane, HALF)
    sends_b = []
    for o, far in partners:
        slot = FAR - o
        copy = remote(
            fbuf.at[FAR, mine],
            fbuf.at[slot, mine],
            send_b.at[FAR + o, int(far)],
            recv_b.at[slot, int(far)],
            o,
            far,
        )
        copy.start()
        sends_b.append(copy)

    for o in (1, -1, 2, -2, 3, -3):
        for a in range(2):
            sends_n[(-o, a)].wait_recv()
        build_codes(FAR + o)

    own_part = {}
    next_part = {}
    recv_of = {(o, far): copy for (o, far), copy in zip(partners, sends_b)}
    for o in (0, 1, -1, 2, -2, 3, -3):
        slot = FAR + o
        for group in WAITS.get(o, ()):
            for far in (False, True):
                if (-group, far) in recv_of:
                    recv_of[(-group, far)].wait_recv()
        forces = jnp.concatenate([fbuf[slot, b] for b in range(NB)], axis=1)
        parts = two_parts(forces)
        total = jnp.zeros((96, BLK), F32)
        for e in range(2):
            span = slice(e * SEG, (e + 1) * SEG)
            mask = mask16[slot, :, span] > 0.5
            stack = [
                jnp.where(mask, jnp.broadcast_to(part[k : k + 1], (16, SEG)), 0.0)
                for part in parts
                for k in range(3)
            ]
            total = total + lax.dot_general(
                jnp.concatenate(stack, axis=0).astype(BF16),
                onehot[slot, :, span],
                NT,
                preferred_element_type=F32,
            )
        total = total[0:48] + total[48:96]
        own_part[o] = [total[16 * k : 16 * k + 8] for k in range(3)]
        next_part[o] = [total[16 * k + 8 : 16 * k + 16] for k in range(3)]

    for o in range(-WIDE, FAR + 1):
        eff_o = jnp.concatenate([fbuf[FAR + o, b, 3:4, :] for b in range(NB)], axis=0)
        for k in range(3):
            value = eff_o * (own_part[o][k] + next_part[o - 1][k])
            vel[FAR + o, k] = value
            if o == 0:
                for b in range(NB):
                    velocity_out[k : k + 1, b * BLK : (b + 1) * BLK] = value[b : b + 1, :]

    shift = None
    for o in (0, 1, -1, 2, -2):
        slot = FAR + o
        s = WIDE + o
        moved = [zeros, zeros, zeros]
        for e in range(2):
            code = codes_d[slot, e]
            low = jnp.bitwise_and(code, BLK - 1)
            high = lax.shift_right_logical(code, 7)
            picked = [zeros, zeros, zeros]
            for h in range(16):
                here = high == h
                for k in range(3):
                    row = vel[slot + h // NB, k, h % NB : h % NB + 1, :]
                    table = jnp.broadcast_to(row, (NB, BLK))
                    found = jnp.take_along_axis(table, low, axis=1, mode="promise_in_bounds")
                    picked[k] = jnp.where(here, found, picked[k])
            moved = [x + y for x, y in zip(moved, picked)]
        moved = [0.5 * TIME_STEP * x for x in moved]
        if shift is None:
            shift = [
                jnp.sum(jnp.sum(x, axis=1, keepdims=True), axis=0, keepdims=True) / SEG
                for x in moved
            ]
        moved = [x - jnp.broadcast_to(y, (NB, BLK)) for x, y in zip(moved, shift)]
        c, unused, (ch, cm, cl), (sh, sm) = kept_centres[o]
        vh, vl = split2(moved)
        ph, pm = two_parts(dot3(c, moved))
        speed = dot3(moved, moved)
        mh, ml = two_parts(speed + CORE_SQUARE)
        rows = vh + vl + [ph, pm] + vh + vl + [ones, ones]
        rows += ch + cm + [mh, ml] + ch + cm + [sh, sm]
        put(stage_n, s * NB, rows)
        if o == 0:
            kh, kl = two_parts(speed)
            zh, zm = two_parts(dot3(c, c))
            none = [zeros, zeros]
            rows = ch * 2 + [-ones, -ones] + cm * 2 + [-ph, -pm] + vh * 2 + none + vl * 2 + none
            put(stage_t, 0, rows)
            rows = twice(vh) * 2 + none + twice(vl) * 2 + [kh, kl]
            rows += [zeros] * 6 + [ones, ones] + [zeros] * 8
            put(stage_t, NB, rows)
            rows = [zeros] * 14 + [zh, zm] + twice(ch) * 2 + none + twice(cm) * 2 + [ones, ones]
            put(stage_t, 2 * NB, rows)
            for b in range(NB):
                for g in range(3):
                    rows_of = pl.ds(33 * (g * NB + b), 32)
                    goal[b, :, g * BLK : (g + 1) * BLK] = stage_t[rows_of, :].astype(BF16)

    block_rows = lax.broadcasted_iota(jnp.int32, (NB, BLK), 0)

    def some_pairs(n, near):
        for step in range(TOGETHER):
            into = cand_t[TOGETHER * n + step]
            source = cand_s[TOGETHER * n + step]
            there = jnp.transpose(stage_n[pl.ds(source * 33, 32), :])
            both = lax.dot_general(
                there.astype(BF16), goal[into], NN, preferred_element_type=F32
            )
            ahead = both[:, 0:BLK]
            square = both[:, BLK : 2 * BLK]
            kept = jnp.minimum(jnp.maximum(ahead, 0.0), square)
            fraction = kept / square
            near_by = jnp.exp(
                fraction * (2.0 * ahead - kept + CORE_SQUARE * fraction) - both[:, 2 * BLK :]
            )
            row = jnp.sum(near_by, axis=0, keepdims=True)
            near = near + jnp.where(block_rows == into, jnp.broadcast_to(row, (NB, BLK)), 0.0)
        return near

    near = lax.fori_loop(0, NCAND // TOGETHER, some_pairs, jnp.zeros((NB, BLK), F32))
    nearness_out[...] = math.exp(CORE_SQUARE) * near

    for copy in list(sends_a.values()) + list(sends_n.values()) + sends_b + [list_copy, drag_copy]:
        copy.wait_send()


def local(
    centres,
    seg_lines,
    burgers,
    neighbour_blocks,
    seg_nodes,
    node_owner,
    mobility,
    cand_target,
    cand_source,
):
    n_cells = lax.axis_size("cells")
    window = 2 * WIDE + 1
    anywhere = pl.BlockSpec(memory_space=pl.ANY)
    vmem = pl.BlockSpec(memory_space=pltpu.VMEM)
    smem = pl.BlockSpec(memory_space=pltpu.SMEM)
    velocity, nearness = pl.pallas_call(
        functools.partial(kernel, n_cells),
        name="dislocation_step",
        out_shape=(
            jax.ShapeDtypeStruct((3, SEG), F32),
            jax.ShapeDtypeStruct((NB, BLK), F32),
        ),
        in_specs=[anywhere, smem, smem] + [anywhere] * 5 + [vmem],
        out_specs=(vmem, vmem),
        scratch_shapes=[
            pltpu.VMEM((window, 3, SEG), F32),
            pltpu.VMEM((window, 3, SEG), F32),
            pltpu.VMEM((window, 3, SEG), F32),
            pltpu.VMEM((SPAN, 2, SEG), jnp.int32),
            pltpu.VMEM((SPAN, 2, SEG), jnp.int32),
            pltpu.SMEM((NB, NENT), jnp.int32),
            pltpu.VMEM((NB, NENT), jnp.int32),
            pltpu.SMEM((NB, NENT), jnp.int32),
            pltpu.VMEM((window, 72, BLK), F32),
            pltpu.VMEM((window * NB * 49, BLK), F32),
            pltpu.VMEM((window * NB * 17, BLK), F32),
            pltpu.VMEM((NB * 25, BLK), F32),
            pltpu.VMEM((NB * 17, BLK), F32),
            pltpu.VMEM((window * NB * 33, BLK), F32),
            pltpu.VMEM((3 * NB * 33, BLK), F32),
            pltpu.VMEM((window * NB, 48, BLK), BF16),
            pltpu.VMEM((window * NB, 16, BLK), BF16),
            pltpu.VMEM((NB, 2 * BLK, 48), BF16),
            pltpu.VMEM((NB, 32, 3 * BLK), BF16),
            pltpu.VMEM((SPAN, 2, NB, BLK), jnp.int32),
            pltpu.VMEM((SPAN, BLK, 2 * SEG), BF16),
            pltpu.VMEM((SPAN, 16, 2 * SEG), F32),
            pltpu.VMEM((NB, BLK), F32),
            pltpu.VMEM((NB, BLK), F32),
            pltpu.VMEM((NB, 1, BLK), F32),
            pltpu.VMEM((SPAN, NB, 4, BLK), F32),
            pltpu.VMEM((SPAN, 3, NB, BLK), F32),
            pltpu.SemaphoreType.DMA((6,)),
            pltpu.SemaphoreType.DMA((window, 3)),
            pltpu.SemaphoreType.DMA((window, 3)),
            pltpu.SemaphoreType.DMA((SPAN, 2)),
            pltpu.SemaphoreType.DMA((SPAN, 2)),
            pltpu.SemaphoreType.DMA((5,)),
            pltpu.SemaphoreType.DMA((SPAN, 2)),
            pltpu.SemaphoreType.DMA((SPAN, 2)),
        ],
        compiler_params=pltpu.CompilerParams(
            collective_id=0, has_side_effects=True, vmem_limit_bytes=60 * 1024 * 1024
        ),
    )(
        neighbour_blocks,
        cand_target,
        cand_source,
        centres,
        seg_lines,
        burgers,
        seg_nodes,
        node_owner,
        mobility.reshape(NB, BLK),
    )
    return velocity, nearness.reshape(SEG)


def solution(mesh):
    in_specs = (
        P(None, "cells"),
        P(None, "cells"),
        P(None, "cells"),
        P("cells", "lanes"),
        P(None, "cells"),
        P(None, "cells"),
        P("cells"),
        P("cells"),
        P("cells"),
    )
    out_specs = (P(None, "cells"), P("cells"))
    return jax.shard_map(local, mesh=mesh, in_specs=in_specs, out_specs=out_specs, check_vma=False)
```

```python
import functools
import math

import jax
import jax.numpy as jnp
from jax import lax
from jax.experimental import pallas as pl
from jax.experimental.pallas import tpu as pltpu
from jax.sharding import PartitionSpec as P

BLK = 128
NB = 8
SEG = BLK * NB
HALF = NB // 2
NENT = 8
NCAND = 32
WIDE = 2
FAR = 3
SPAN = 2 * FAR + 1
FORCE_SCALE = 0.02
CORE_SQUARE = 0.25
TIME_STEP = 4.0
CENTRE = 2.0
TOGETHER = 8
AHEAD = 8
F32 = jnp.float32
BF16 = jnp.bfloat16
MESH = pl.DeviceIdType.MESH
NT = (((1,), (1,)), ((), ()))
NN = (((1,), (0,)), ((), ()))


def rounded(x):
    return x.astype(BF16).astype(F32)


def two_parts(x):
    top = rounded(x)
    return top, rounded(x - top)


def three_parts(x):
    top = rounded(x)
    rest = x - top
    mid = rounded(rest)
    return top, mid, rounded(rest - mid)


def kernel(
    n_cells,
    lists_hbm,
    cand_t_hbm,
    cand_s_hbm,
    centres_hbm,
    lines_hbm,
    burgers_hbm,
    nodes_hbm,
    owner_hbm,
    mobility_hbm,
    velocity_out,
    nearness_out,
    win_c,
    win_l,
    win_b,
    codes_n,
    codes_o,
    cand_t,
    cand_s,
    mobility,
    list_own,
    list_far_v,
    list_far,
    dense,
    stage_f,
    stage_p,
    stage_q,
    stage_a,
    stage_n,
    stage_t,
    feat,
    pull,
    target,
    goal,
    codes_d,
    onehot,
    mask16,
    drag_send,
    drag_recv,
    eff,
    fbuf,
    vel,
    local_sem,
    send_a,
    recv_a,
    send_n,
    recv_n,
    misc_sem,
    send_b,
    recv_b,
):
    me = lax.axis_index("cells")
    lane = lax.axis_index("lanes")
    other = 1 - lane

    def cell(offset):
        return lax.rem(me + (offset + n_cells), n_cells)

    partners = [
        (o, far) for o in (0, 1, -1, 2, -2, 3, -3) for far in (False, True) if (o, far) != (0, False)
    ]

    greeted = [(o, False) for o in (3, -3, 2, -2, 1, -1)] + [(0, True)]
    barrier = pltpu.get_barrier_semaphore()
    for o, far in greeted:
        pl.semaphore_signal(
            barrier, inc=1, device_id=(cell(o), other if far else lane), device_id_type=MESH
        )
    own_copies = [
        pltpu.make_async_copy(centres_hbm, win_c.at[WIDE], local_sem.at[0]),
        pltpu.make_async_copy(lines_hbm, win_l.at[WIDE], local_sem.at[1]),
        pltpu.make_async_copy(burgers_hbm, win_b.at[WIDE], local_sem.at[2]),
        pltpu.make_async_copy(nodes_hbm, codes_n.at[FAR], local_sem.at[3]),
        pltpu.make_async_copy(owner_hbm, codes_o.at[FAR], local_sem.at[4]),
        pltpu.make_async_copy(lists_hbm, list_own, local_sem.at[5]),
        pltpu.make_async_copy(mobility_hbm, mobility, local_sem.at[6]),
        pltpu.make_async_copy(cand_t_hbm, cand_t, local_sem.at[7]),
        pltpu.make_async_copy(cand_s_hbm, cand_s, local_sem.at[8]),
    ]
    for copy in own_copies:
        copy.start()
    pl.semaphore_wait(barrier, len(greeted))

    def remote(src, dst, send, recv, o, far):
        return pltpu.make_async_remote_copy(
            src_ref=src,
            dst_ref=dst,
            send_sem=send,
            recv_sem=recv,
            device_id=(cell(o), other if far else lane),
            device_id_type=MESH,
        )

    sends_a = {}
    for o in (1, -1, 2, -2):
        for a, (src, dst) in enumerate(
            ((centres_hbm, win_c), (lines_hbm, win_l), (burgers_hbm, win_b))
        ):
            slot = WIDE - o
            sends_a[(o, a)] = remote(
                src, dst.at[slot], send_a.at[WIDE + o, a], recv_a.at[slot, a], o, False
            )
            sends_a[(o, a)].start()
    list_copy = remote(lists_hbm, list_far_v, misc_sem.at[0], misc_sem.at[1], 0, True)
    list_copy.start()
    sends_n = {}
    for o in (1, -1, 2, -2, 3, -3):
        for a, (src, dst) in enumerate(((nodes_hbm, codes_n), (owner_hbm, codes_o))):
            slot = FAR - o
            sends_n[(o, a)] = remote(
                src, dst.at[slot], send_n.at[FAR + o, a], recv_n.at[slot, a], o, False
            )
            sends_n[(o, a)].start()
    for copy in own_copies:
        copy.wait()

    def build_codes(slot):
        for e in range(2):
            node = codes_n[slot, e : e + 1, :] + SEG * codes_o[slot, e : e + 1, :]
            low = jnp.bitwise_and(node, BLK - 1)
            high = lax.shift_right_logical(node, 7)
            span = pl.ds(e * SEG, SEG)
            rows = lax.broadcasted_iota(jnp.int32, (BLK, SEG), 0)
            onehot[slot, :, span] = (rows == low).astype(F32).astype(BF16)
            rows16 = lax.broadcasted_iota(jnp.int32, (16, SEG), 0)
            mask16[slot, :, span] = (rows16 == high).astype(F32)
            for b in range(NB):
                codes_d[slot, e, b : b + 1, :] = node[:, b * BLK : (b + 1) * BLK]

    ones = jnp.ones((NB, BLK), F32)
    zeros = jnp.zeros((NB, BLK), F32)

    def odd(rows):
        return len(rows) | 1

    def put(ref, base, rows):
        for r, row in enumerate(rows):
            ref[pl.ds(base * odd(rows) + r, NB, stride=odd(rows)), :] = row

    def dense_fields(s):
        for a, win in enumerate((win_c, win_l, win_b)):
            for b in range(NB):
                dense[s, pl.ds(24 * a + b, 3, stride=NB), :] = win[s, :, b * BLK : (b + 1) * BLK]
        parts = [dense[s, NB * k : NB * (k + 1), :] for k in range(9)]
        return [x - CENTRE for x in parts[0:3]], parts[3:6], parts[6:9]

    def dot3(x, y):
        return x[0] * y[0] + x[1] * y[1] + x[2] * y[2]

    def split3(rows):
        return [list(x) for x in zip(*(three_parts(row) for row in rows))]

    def split2(rows):
        return [list(x) for x in zip(*(two_parts(row) for row in rows))]

    def build_source(s):
        c, line, burg = dense_fields(s)
        ch, cm, cl = split3(c)
        sh, sm, sl = three_parts(dot3(c, c) + CORE_SQUARE)
        bh, bm = split2(burg)
        rows = ch + cm + [sh, sm] + ch + cm + [ones, ones] + cl + ch + [sl, ones]
        rows += (bh + bm + [zeros, zeros]) * 2 + [zeros] * 8
        put(stage_f, s * NB, rows)
        moment = [
            line[1] * c[2] - line[2] * c[1],
            line[2] * c[0] - line[0] * c[2],
            line[0] * c[1] - line[1] * c[0],
        ]
        high, low = split2(line + moment)
        put(stage_p, s * NB, high + [zeros, zeros] + low + [zeros, zeros])
        for b in range(s * NB, (s + 1) * NB):
            feat[b] = jnp.transpose(stage_f[49 * b : 49 * b + 48, :]).astype(BF16)
            pulls = stage_p[17 * b : 17 * b + 16, :].astype(BF16)
            pull[b] = jnp.concatenate([pulls, pulls], axis=1)
        return c, line, (ch, cm, cl), (sh, sm)

    centre_own, line_own, (ch, cm, cl), own_square = build_source(WIDE)

    def twice(rows):
        return [-2.0 * row for row in rows]

    zh, zm, zl = three_parts(dot3(centre_own, centre_own))
    lh, lm = split2(line_own)
    rows = twice(ch) * 2 + [ones, ones] + twice(cm) * 2 + [zh, zm]
    rows += twice(ch) + twice(cl) + [ones, zl]
    put(stage_q, 0, rows)
    put(stage_a, 0, lh * 2 + [zeros, zeros] + lm * 2 + [zeros, zeros])
    for b in range(NB):
        right = jnp.concatenate([stage_q[25 * b : 25 * b + 24, :], jnp.zeros((24, BLK), F32)], 0)
        target[b, :, 0:BLK] = right.astype(BF16)
        right = jnp.concatenate(
            [
                jnp.zeros((24, BLK), F32),
                stage_a[17 * b : 17 * b + 16, :],
                jnp.zeros((8, BLK), F32),
            ],
            0,
        )
        target[b, :, BLK : 2 * BLK] = right.astype(BF16)

    build_codes(FAR)
    line = [win_l[WIDE, k : k + 1, :] for k in range(3)]
    length = 0.5 * jnp.sqrt(dot3(line, line))
    drag = jnp.zeros((32, BLK), F32)
    for e in range(2):
        span = slice(e * SEG, (e + 1) * SEG)
        mask = mask16[FAR, :, span] > 0.5
        parts = [
            jnp.where(mask, jnp.broadcast_to(part, (16, SEG)), 0.0) for part in two_parts(length)
        ]
        drag = drag + lax.dot_general(
            jnp.concatenate(parts, axis=0).astype(BF16),
            onehot[FAR, :, span],
            NT,
            preferred_element_type=F32,
        )
    drag_send[...] = drag[8:16] + drag[24:32]
    drag_copy = remote(drag_send, drag_recv, misc_sem.at[2], misc_sem.at[3], 1, False)
    drag_copy.start()
    own_drag = drag[0:8] + drag[16:24]

    kept_centres = {0: (centre_own, line_own, (ch, cm, cl), own_square)}
    for o in (1, -1, 2, -2):
        for a in range(3):
            sends_a[(-o, a)].wait_recv()
        kept_centres[o] = build_source(WIDE + o)
    list_copy.wait_recv()
    to_smem = pltpu.make_async_copy(list_far_v, list_far, misc_sem.at[4])
    to_smem.start()
    to_smem.wait()
    drag_copy.wait_recv()
    eff_all = mobility[...] / (1.0 + (own_drag + drag_recv[...]))
    for b in range(NB):
        eff[b] = eff_all[b : b + 1, :]

    def one_target(t, carry):
        block = HALF * lane + t
        right = target[block]
        total = jnp.zeros((16, BLK), F32)
        sources = [lists[block, e] for lists in (list_own, list_far) for e in range(NENT)]
        ahead = []
        for n in range(len(sources) + AHEAD):
            if n < len(sources):
                ahead.append(
                    lax.dot_general(feat[sources[n]], right, NN, preferred_element_type=F32)
                )
            if n < AHEAD:
                continue
            both = ahead[n - AHEAD]
            inverse = lax.rsqrt(both[:, 0:BLK])
            weight = both[:, BLK : 2 * BLK] * inverse * inverse * inverse
            top = weight.astype(BF16)
            low = (weight - top.astype(F32)).astype(BF16)
            total = total + lax.dot_general(
                pull[sources[n - AHEAD]],
                jnp.concatenate([top, low], axis=0),
                NN,
                preferred_element_type=F32,
            )
        total = total[0:8] + total[8:16]
        cut = pl.ds(pl.multiple_of(block * BLK, BLK), BLK)
        x, y, z = (win_c[WIDE, k : k + 1, cut] - CENTRE for k in range(3))
        sx, sy, sz = (total[k : k + 1] for k in range(3))
        scale = 0.5 * FORCE_SCALE
        fbuf[FAR, block, 0:1, :] = scale * (sy * z - sz * y - total[3:4])
        fbuf[FAR, block, 1:2, :] = scale * (sz * x - sx * z - total[4:5])
        fbuf[FAR, block, 2:3, :] = scale * (sx * y - sy * x - total[5:6])
        fbuf[FAR, block, 3:4, :] = eff[block]
        return carry

    lax.fori_loop(0, HALF, one_target, 0)

    for copy in sends_n.values():
        copy.wait_recv()

    mine = pl.ds(HALF * lane, HALF)
    sends_b = []
    for o, far in partners:
        slot = FAR - o
        copy = remote(
            fbuf.at[FAR, mine],
            fbuf.at[slot, mine],
            send_b.at[FAR + o, int(far)],
            recv_b.at[slot, int(far)],
            o,
            far,
        )
        copy.start()
        sends_b.append(copy)

    for o in (1, -1, 2, -2, 3, -3):
        build_codes(FAR + o)
    for copy in list(sends_a.values()) + list(sends_n.values()) + [list_copy, drag_copy]:
        copy.wait_send()

    own_part = {}
    next_part = {}
    recv_of = dict(zip(partners, sends_b))

    def wait_forces(o):
        for far in (False, True):
            if (-o, far) in recv_of:
                recv_of[(-o, far)].wait_recv()

    def scatter(o):
        slot = FAR + o
        forces = jnp.concatenate([fbuf[slot, b] for b in range(NB)], axis=1)
        parts = two_parts(forces)
        first = NB if o == -FAR else 0
        last = NB if o == FAR else 2 * NB
        size = last - first
        total = jnp.zeros((6 * size, BLK), F32)
        for e in range(2):
            span = slice(e * SEG, (e + 1) * SEG)
            mask = mask16[slot, first:last, span] > 0.5
            stack = [
                jnp.where(mask, jnp.broadcast_to(part[k : k + 1], (size, SEG)), 0.0)
                for part in parts
                for k in range(3)
            ]
            total = total + lax.dot_general(
                jnp.concatenate(stack, axis=0).astype(BF16),
                onehot[slot, :, span],
                NT,
                preferred_element_type=F32,
            )
        total = total[0 : 3 * size] + total[3 * size : 6 * size]
        if o < FAR:
            next_part[o] = [total[size * (k + 1) - NB : size * (k + 1)] for k in range(3)]
        if o > -FAR:
            own_part[o] = [total[size * k : size * k + NB] for k in range(3)]

    def node_velocity(o):
        eff_o = jnp.concatenate([fbuf[FAR + o, b, 3:4, :] for b in range(NB)], axis=0)
        for k in range(3):
            value = eff_o * (own_part[o][k] + next_part[o - 1][k])
            vel[FAR + o, k] = value
            if o == 0:
                for b in range(NB):
                    velocity_out[k : k + 1, b * BLK : (b + 1) * BLK] = value[b : b + 1, :]

    shift = []

    def gather(o):
        slot = FAR + o
        s = WIDE + o
        moved = [zeros, zeros, zeros]
        for e in range(2):
            code = codes_d[slot, e]
            low = jnp.bitwise_and(code, BLK - 1)
            high = lax.shift_right_logical(code, 7)
            picked = [zeros, zeros, zeros]
            for h in range(16):
                here = high == h
                for k in range(3):
                    row = vel[slot + h // NB, k, h % NB : h % NB + 1, :]
                    table = jnp.broadcast_to(row, (NB, BLK))
                    found = jnp.take_along_axis(table, low, axis=1, mode="promise_in_bounds")
                    picked[k] = jnp.where(here, found, picked[k])
            moved = [x + y for x, y in zip(moved, picked)]
        moved = [0.5 * TIME_STEP * x for x in moved]
        if not shift:
            shift.extend(
                jnp.sum(jnp.sum(x, axis=1, keepdims=True), axis=0, keepdims=True) / SEG
                for x in moved
            )
        moved = [x - jnp.broadcast_to(y, (NB, BLK)) for x, y in zip(moved, shift)]
        c, unused, (ch, cm, cl), (sh, sm) = kept_centres[o]
        vh, vl = split2(moved)
        ph, pm = two_parts(dot3(c, moved))
        speed = dot3(moved, moved)
        mh, ml = two_parts(speed + CORE_SQUARE)
        rows = vh + vl + [ph, pm] + vh + vl + [ones, ones]
        rows += ch + cm + [mh, ml] + ch + cm + [sh, sm]
        put(stage_n, s * NB, rows)
        if o == 0:
            kh, kl = two_parts(speed)
            zh, zm = two_parts(dot3(c, c))
            none = [zeros, zeros]
            rows = ch * 2 + [-ones, -ones] + cm * 2 + [-ph, -pm] + vh * 2 + none + vl * 2 + none
            put(stage_t, 0, rows)
            rows = twice(vh) * 2 + none + twice(vl) * 2 + [kh, kl]
            rows += [zeros] * 6 + [ones, ones] + [zeros] * 8
            put(stage_t, NB, rows)
            rows = [zeros] * 14 + [zh, zm] + twice(ch) * 2 + none + twice(cm) * 2 + [ones, ones]
            put(stage_t, 2 * NB, rows)
            for b in range(NB):
                for g in range(3):
                    rows_of = pl.ds(33 * (g * NB + b), 32)
                    goal[b, :, g * BLK : (g + 1) * BLK] = stage_t[rows_of, :].astype(BF16)

    for o in (0, 1, 2, 3):
        wait_forces(o)
    for o in (0, 1, 2, 3):
        scatter(o)
    for o in (1, 2, 3):
        node_velocity(o)
    for o in (1, 2):
        gather(o)
    for o in (-1, -2, -3):
        wait_forces(o)
    for o in (-1, -2, -3):
        scatter(o)
    for o in (0, -1, -2):
        node_velocity(o)
    for o in (0, -1, -2):
        gather(o)

    block_rows = lax.broadcasted_iota(jnp.int32, (NB, BLK), 0)

    def some_pairs(n, near):
        for step in range(TOGETHER):
            into = cand_t[TOGETHER * n + step]
            source = cand_s[TOGETHER * n + step]
            there = jnp.transpose(stage_n[pl.ds(source * 33, 32), :])
            both = lax.dot_general(
                there.astype(BF16), goal[into], NN, preferred_element_type=F32
            )
            ahead = both[:, 0:BLK]
            square = both[:, BLK : 2 * BLK]
            kept = jnp.minimum(jnp.maximum(ahead, 0.0), square)
            fraction = kept / square
            near_by = jnp.exp(
                fraction * (2.0 * ahead - kept + CORE_SQUARE * fraction) - both[:, 2 * BLK :]
            )
            row = jnp.sum(near_by, axis=0, keepdims=True)
            near = near + jnp.where(block_rows == into, jnp.broadcast_to(row, (NB, BLK)), 0.0)
        return near

    near = lax.fori_loop(0, NCAND // TOGETHER, some_pairs, jnp.zeros((NB, BLK), F32))
    nearness_out[...] = math.exp(CORE_SQUARE) * near

    for copy in sends_b:
        copy.wait_send()


def local(
    centres,
    seg_lines,
    burgers,
    neighbour_blocks,
    seg_nodes,
    node_owner,
    mobility,
    cand_target,
    cand_source,
):
    n_cells = lax.axis_size("cells")
    window = 2 * WIDE + 1
    hbm = pl.BlockSpec(memory_space=pltpu.HBM)
    vmem = pl.BlockSpec(memory_space=pltpu.VMEM)
    velocity, nearness = pl.pallas_call(
        functools.partial(kernel, n_cells),
        name="dislocation_step",
        out_shape=(
            jax.ShapeDtypeStruct((3, SEG), F32),
            jax.ShapeDtypeStruct((NB, BLK), F32),
        ),
        in_specs=[hbm] * 9,
        out_specs=(vmem, vmem),
        scratch_shapes=[
            pltpu.VMEM((window, 3, SEG), F32),
            pltpu.VMEM((window, 3, SEG), F32),
            pltpu.VMEM((window, 3, SEG), F32),
            pltpu.VMEM((SPAN, 2, SEG), jnp.int32),
            pltpu.VMEM((SPAN, 2, SEG), jnp.int32),
            pltpu.SMEM((NCAND,), jnp.int32),
            pltpu.SMEM((NCAND,), jnp.int32),
            pltpu.VMEM((NB, BLK), F32),
            pltpu.SMEM((NB, NENT), jnp.int32),
            pltpu.VMEM((NB, NENT), jnp.int32),
            pltpu.SMEM((NB, NENT), jnp.int32),
            pltpu.VMEM((window, 72, BLK), F32),
            pltpu.VMEM((window * NB * 49, BLK), F32),
            pltpu.VMEM((window * NB * 17, BLK), F32),
            pltpu.VMEM((NB * 25, BLK), F32),
            pltpu.VMEM((NB * 17, BLK), F32),
            pltpu.VMEM((window * NB * 33, BLK), F32),
            pltpu.VMEM((3 * NB * 33, BLK), F32),
            pltpu.VMEM((window * NB, BLK, 48), BF16),
            pltpu.VMEM((window * NB, 16, 2 * BLK), BF16),
            pltpu.VMEM((NB, 48, 2 * BLK), BF16),
            pltpu.VMEM((NB, 32, 3 * BLK), BF16),
            pltpu.VMEM((SPAN, 2, NB, BLK), jnp.int32),
            pltpu.VMEM((SPAN, BLK, 2 * SEG), BF16),
            pltpu.VMEM((SPAN, 16, 2 * SEG), F32),
            pltpu.VMEM((NB, BLK), F32),
            pltpu.VMEM((NB, BLK), F32),
            pltpu.VMEM((NB, 1, BLK), F32),
            pltpu.VMEM((SPAN, NB, 4, BLK), F32),
            pltpu.VMEM((SPAN, 3, NB, BLK), F32),
            pltpu.SemaphoreType.DMA((9,)),
            pltpu.SemaphoreType.DMA((window, 3)),
            pltpu.SemaphoreType.DMA((window, 3)),
            pltpu.SemaphoreType.DMA((SPAN, 2)),
            pltpu.SemaphoreType.DMA((SPAN, 2)),
            pltpu.SemaphoreType.DMA((5,)),
            pltpu.SemaphoreType.DMA((SPAN, 2)),
            pltpu.SemaphoreType.DMA((SPAN, 2)),
        ],
        compiler_params=pltpu.CompilerParams(
            collective_id=0, has_side_effects=True, vmem_limit_bytes=60 * 1024 * 1024
        ),
    )(
        neighbour_blocks,
        cand_target,
        cand_source,
        centres,
        seg_lines,
        burgers,
        seg_nodes,
        node_owner,
        mobility.reshape(NB, BLK),
    )
    return velocity, nearness.reshape(SEG)


def solution(mesh):
    in_specs = (
        P(None, "cells"),
        P(None, "cells"),
        P(None, "cells"),
        P("cells", "lanes"),
        P(None, "cells"),
        P(None, "cells"),
        P("cells"),
        P("cells"),
        P("cells"),
    )
    out_specs = (P(None, "cells"), P("cells"))
    return jax.shard_map(local, mesh=mesh, in_specs=in_specs, out_specs=out_specs, check_vma=False)
```

```python
import functools
import math

import jax
import jax.numpy as jnp
from jax import lax
from jax.experimental import pallas as pl
from jax.experimental.pallas import tpu as pltpu
from jax.sharding import PartitionSpec as P

BLK = 128
NB = 8
SEG = BLK * NB
HALF = NB // 2
NENT = 8
NCAND = 32
WIDE = 2
FAR = 3
SPAN = 2 * FAR + 1
FORCE_SCALE = 0.02
CORE_SQUARE = 0.25
TIME_STEP = 4.0
CENTRE = 2.0
TOGETHER = 16
SOONER = 4
AHEAD = 8
F32 = jnp.float32
BF16 = jnp.bfloat16
MESH = pl.DeviceIdType.MESH
NT = (((1,), (1,)), ((), ()))
NN = (((1,), (0,)), ((), ()))


def rounded(x):
    return x.astype(BF16).astype(F32)


def two_parts(x):
    top = rounded(x)
    return top, rounded(x - top)


def three_parts(x):
    top = rounded(x)
    rest = x - top
    mid = rounded(rest)
    return top, mid, rounded(rest - mid)


def kernel(
    n_cells,
    lists_hbm,
    cand_t_hbm,
    cand_s_hbm,
    centres_hbm,
    lines_hbm,
    burgers_hbm,
    nodes_hbm,
    owner_hbm,
    mobility_hbm,
    velocity_out,
    nearness_out,
    win_c,
    win_l,
    win_b,
    nodes,
    owner,
    codes_r,
    cand_t,
    cand_s,
    mobility,
    list_own,
    list_far_v,
    list_far,
    dense,
    stage_f,
    stage_p,
    stage_q,
    stage_a,
    stage_n,
    stage_t,
    feat,
    pull,
    target,
    goal,
    codes_d,
    onehot,
    mask16,
    drag_send,
    drag_recv,
    eff,
    fbuf,
    vel,
    local_sem,
    send_a,
    recv_a,
    send_n,
    recv_n,
    misc_sem,
    send_b,
    recv_b,
):
    me = lax.axis_index("cells")
    lane = lax.axis_index("lanes")
    other = 1 - lane

    def cell(offset):
        return lax.rem(me + (offset + n_cells), n_cells)

    partners = [
        (o, far) for o in (0, 1, -1, 2, -2, 3, -3) for far in (False, True) if (o, far) != (0, False)
    ]

    greeted = [(o, False) for o in (3, -3, 2, -2, 1, -1)] + [(0, True)]
    barrier = pltpu.get_barrier_semaphore()
    for o, far in greeted:
        pl.semaphore_signal(
            barrier, inc=1, device_id=(cell(o), other if far else lane), device_id_type=MESH
        )
    own_copies = [
        pltpu.make_async_copy(centres_hbm, win_c, local_sem.at[0]),
        pltpu.make_async_copy(lines_hbm, win_l, local_sem.at[1]),
        pltpu.make_async_copy(burgers_hbm, win_b, local_sem.at[2]),
        pltpu.make_async_copy(nodes_hbm, nodes, local_sem.at[3]),
        pltpu.make_async_copy(owner_hbm, owner, local_sem.at[4]),
        pltpu.make_async_copy(lists_hbm, list_own, local_sem.at[5]),
        pltpu.make_async_copy(mobility_hbm, mobility, local_sem.at[6]),
        pltpu.make_async_copy(cand_t_hbm, cand_t, local_sem.at[7]),
        pltpu.make_async_copy(cand_s_hbm, cand_s, local_sem.at[8]),
    ]
    for copy in own_copies:
        copy.start()
    for copy in own_copies:
        copy.wait()

    for a, win in enumerate((win_c, win_l, win_b)):
        for b in range(NB):
            dense[WIDE, pl.ds(24 * a + b, 3, stride=NB), :] = win[:, b * BLK : (b + 1) * BLK]
    codes_r[FAR] = nodes[...] + SEG * owner[...]
    pl.semaphore_wait(barrier, len(greeted))

    def remote(src, dst, send, recv, o, far):
        return pltpu.make_async_remote_copy(
            src_ref=src,
            dst_ref=dst,
            send_sem=send,
            recv_sem=recv,
            device_id=(cell(o), other if far else lane),
            device_id_type=MESH,
        )

    list_copy = remote(lists_hbm, list_far_v, misc_sem.at[0], misc_sem.at[1], 0, True)
    list_copy.start()
    sends_a = {}
    for o in (-2, -1, 2, 1):
        slot = WIDE - o
        sends_a[o] = remote(
            dense.at[WIDE], dense.at[slot], send_a.at[WIDE + o], recv_a.at[slot], o, False
        )
        sends_a[o].start()
    sends_n = {}
    for o in (-3, -2, -1, 3, 2, 1):
        slot = FAR - o
        sends_n[o] = remote(
            codes_r.at[FAR], codes_r.at[slot], send_n.at[FAR + o], recv_n.at[slot], o, False
        )
        sends_n[o].start()

    def build_codes(slot):
        for e in range(2):
            node = codes_r[slot, e : e + 1, :]
            low = jnp.bitwise_and(node, BLK - 1)
            high = lax.shift_right_logical(node, 7)
            span = pl.ds(e * SEG, SEG)
            rows = lax.broadcasted_iota(jnp.int32, (BLK, SEG), 0)
            onehot[slot, :, span] = (rows == low).astype(F32).astype(BF16)
            rows16 = lax.broadcasted_iota(jnp.int32, (16, SEG), 0)
            mask16[slot, :, span] = (rows16 == high).astype(F32)
            for b in range(NB):
                codes_d[slot, e, b : b + 1, :] = node[:, b * BLK : (b + 1) * BLK]

    ones = jnp.ones((NB, BLK), F32)
    zeros = jnp.zeros((NB, BLK), F32)

    def odd(rows):
        return len(rows) | 1

    def put(ref, base, rows):
        for r, row in enumerate(rows):
            ref[pl.ds(base * odd(rows) + r, NB, stride=odd(rows)), :] = row

    def dense_fields(s):
        parts = [dense[s, NB * k : NB * (k + 1), :] for k in range(9)]
        return [x - CENTRE for x in parts[0:3]], parts[3:6], parts[6:9]

    def dot3(x, y):
        return x[0] * y[0] + x[1] * y[1] + x[2] * y[2]

    def split3(rows):
        return [list(x) for x in zip(*(three_parts(row) for row in rows))]

    def split2(rows):
        return [list(x) for x in zip(*(two_parts(row) for row in rows))]

    def build_source(s):
        c, line, burg = dense_fields(s)
        ch, cm, cl = split3(c)
        sh, sm, sl = three_parts(dot3(c, c) + CORE_SQUARE)
        bh, bm = split2(burg)
        rows = ch + cm + [sh, sm] + ch + cm + [ones, ones] + cl + ch + [sl, ones]
        rows += (bh + bm + [zeros, zeros]) * 2 + [zeros] * 8
        put(stage_f, s * NB, rows)
        moment = [
            line[1] * c[2] - line[2] * c[1],
            line[2] * c[0] - line[0] * c[2],
            line[0] * c[1] - line[1] * c[0],
        ]
        high, low = split2(line + moment)
        put(stage_p, s * NB, high + [zeros, zeros] + low + [zeros, zeros])
        for b in range(s * NB, (s + 1) * NB):
            feat[b] = jnp.transpose(stage_f[49 * b : 49 * b + 48, :]).astype(BF16)
            pulls = stage_p[17 * b : 17 * b + 16, :].astype(BF16)
            pull[b] = jnp.concatenate([pulls, pulls], axis=1)
        return c, line, (ch, cm, cl), (sh, sm)

    centre_own, line_own, (ch, cm, cl), own_square = build_source(WIDE)

    def twice(rows):
        return [-2.0 * row for row in rows]

    zh, zm, zl = three_parts(dot3(centre_own, centre_own))
    lh, lm = split2(line_own)
    rows = twice(ch) * 2 + [ones, ones] + twice(cm) * 2 + [zh, zm]
    rows += twice(ch) + twice(cl) + [ones, zl]
    put(stage_q, 0, rows)
    put(stage_a, 0, lh * 2 + [zeros, zeros] + lm * 2 + [zeros, zeros])
    for b in range(NB):
        right = jnp.concatenate([stage_q[25 * b : 25 * b + 24, :], jnp.zeros((24, BLK), F32)], 0)
        target[b, :, 0:BLK] = right.astype(BF16)
        right = jnp.concatenate(
            [
                jnp.zeros((24, BLK), F32),
                stage_a[17 * b : 17 * b + 16, :],
                jnp.zeros((8, BLK), F32),
            ],
            0,
        )
        target[b, :, BLK : 2 * BLK] = right.astype(BF16)

    build_codes(FAR)
    line = [win_l[k : k + 1, :] for k in range(3)]
    length = 0.5 * jnp.sqrt(dot3(line, line))
    drag = jnp.zeros((32, BLK), F32)
    for e in range(2):
        span = slice(e * SEG, (e + 1) * SEG)
        mask = mask16[FAR, :, span] > 0.5
        parts = [
            jnp.where(mask, jnp.broadcast_to(part, (16, SEG)), 0.0) for part in two_parts(length)
        ]
        drag = drag + lax.dot_general(
            jnp.concatenate(parts, axis=0).astype(BF16),
            onehot[FAR, :, span],
            NT,
            preferred_element_type=F32,
        )
    drag_send[...] = drag[8:16] + drag[24:32]
    drag_copy = remote(drag_send, drag_recv, misc_sem.at[2], misc_sem.at[3], 1, False)
    drag_copy.start()
    own_drag = drag[0:8] + drag[16:24]

    kept_centres = {0: (centre_own, line_own, (ch, cm, cl), own_square)}
    for o in (1, -1, 2, -2):
        sends_a[-o].wait_recv()
        kept_centres[o] = build_source(WIDE + o)
    list_copy.wait_recv()
    to_smem = pltpu.make_async_copy(list_far_v, list_far, misc_sem.at[4])
    to_smem.start()
    to_smem.wait()
    drag_copy.wait_recv()
    eff_all = mobility[...] / (1.0 + (own_drag + drag_recv[...]))
    for b in range(NB):
        eff[b] = eff_all[b : b + 1, :]

    def one_target(t, carry):
        block = HALF * lane + t
        right = target[block]
        total = jnp.zeros((16, BLK), F32)
        sources = [lists[block, e] for lists in (list_own, list_far) for e in range(NENT)]
        ahead = []
        for n in range(len(sources) + AHEAD):
            if n < len(sources):
                ahead.append(
                    lax.dot_general(feat[sources[n]], right, NN, preferred_element_type=F32)
                )
            if n < AHEAD:
                continue
            both = ahead[n - AHEAD]
            inverse = lax.rsqrt(both[:, 0:BLK])
            weight = both[:, BLK : 2 * BLK] * inverse * inverse * inverse
            top = weight.astype(BF16)
            low = (weight - top.astype(F32)).astype(BF16)
            total = total + lax.dot_general(
                pull[sources[n - AHEAD]],
                jnp.concatenate([top, low], axis=0),
                NN,
                preferred_element_type=F32,
            )
        total = total[0:8] + total[8:16]
        cut = pl.ds(pl.multiple_of(block * BLK, BLK), BLK)
        x, y, z = (win_c[k : k + 1, cut] - CENTRE for k in range(3))
        sx, sy, sz = (total[k : k + 1] for k in range(3))
        scale = 0.5 * FORCE_SCALE
        fbuf[FAR, block, 0:1, :] = scale * (sy * z - sz * y - total[3:4])
        fbuf[FAR, block, 1:2, :] = scale * (sz * x - sx * z - total[4:5])
        fbuf[FAR, block, 2:3, :] = scale * (sx * y - sy * x - total[5:6])
        fbuf[FAR, block, 3:4, :] = eff[block]
        return carry

    lax.fori_loop(0, HALF, one_target, 0)

    for copy in sends_n.values():
        copy.wait_recv()

    mine = pl.ds(HALF * lane, HALF)
    sends_b = []
    for o, far in partners:
        slot = FAR - o
        copy = remote(
            fbuf.at[FAR, mine],
            fbuf.at[slot, mine],
            send_b.at[FAR + o, int(far)],
            recv_b.at[slot, int(far)],
            o,
            far,
        )
        copy.start()
        sends_b.append(copy)

    for o in (1, -1, 2, -2, 3, -3):
        build_codes(FAR + o)
    for copy in list(sends_a.values()) + list(sends_n.values()) + [list_copy, drag_copy]:
        copy.wait_send()

    own_part = {}
    next_part = {}
    recv_of = dict(zip(partners, sends_b))

    def wait_forces(o):
        for far in (False, True):
            if (-o, far) in recv_of:
                recv_of[(-o, far)].wait_recv()

    def scatter(o):
        slot = FAR + o
        forces = jnp.concatenate([fbuf[slot, b] for b in range(NB)], axis=1)
        parts = two_parts(forces)
        first = NB if o == -FAR else 0
        last = NB if o == FAR else 2 * NB
        size = last - first
        total = jnp.zeros((6 * size, BLK), F32)
        for e in range(2):
            span = slice(e * SEG, (e + 1) * SEG)
            mask = mask16[slot, first:last, span] > 0.5
            stack = [
                jnp.where(mask, jnp.broadcast_to(part[k : k + 1], (size, SEG)), 0.0)
                for part in parts
                for k in range(3)
            ]
            total = total + lax.dot_general(
                jnp.concatenate(stack, axis=0).astype(BF16),
                onehot[slot, :, span],
                NT,
                preferred_element_type=F32,
            )
        total = total[0 : 3 * size] + total[3 * size : 6 * size]
        if o < FAR:
            next_part[o] = [total[size * (k + 1) - NB : size * (k + 1)] for k in range(3)]
        if o > -FAR:
            own_part[o] = [total[size * k : size * k + NB] for k in range(3)]

    def node_velocity(o):
        eff_o = jnp.concatenate([fbuf[FAR + o, b, 3:4, :] for b in range(NB)], axis=0)
        for k in range(3):
            value = eff_o * (own_part[o][k] + next_part[o - 1][k])
            vel[FAR + o, k] = value
            if o == 0:
                for b in range(NB):
                    velocity_out[k : k + 1, b * BLK : (b + 1) * BLK] = value[b : b + 1, :]

    shift = []

    def gather(o):
        slot = FAR + o
        s = WIDE + o
        moved = [zeros, zeros, zeros]
        for e in range(2):
            code = codes_d[slot, e]
            low = jnp.bitwise_and(code, BLK - 1)
            high = lax.shift_right_logical(code, 7)
            picked = [zeros, zeros, zeros]
            for h in range(16):
                here = high == h
                for k in range(3):
                    row = vel[slot + h // NB, k, h % NB : h % NB + 1, :]
                    table = jnp.broadcast_to(row, (NB, BLK))
                    found = jnp.take_along_axis(table, low, axis=1, mode="promise_in_bounds")
                    picked[k] = jnp.where(here, found, picked[k])
            moved = [x + y for x, y in zip(moved, picked)]
        moved = [0.5 * TIME_STEP * x for x in moved]
        if not shift:
            shift.extend(
                jnp.sum(jnp.sum(x, axis=1, keepdims=True), axis=0, keepdims=True) / SEG
                for x in moved
            )
        moved = [x - jnp.broadcast_to(y, (NB, BLK)) for x, y in zip(moved, shift)]
        c, unused, (ch, cm, cl), (sh, sm) = kept_centres[o]
        vh, vl = split2(moved)
        ph, pm = two_parts(dot3(c, moved))
        speed = dot3(moved, moved)
        mh, ml = two_parts(speed + CORE_SQUARE)
        rows = vh + vl + [ph, pm] + vh + vl + [ones, ones]
        rows += ch + cm + [mh, ml] + ch + cm + [sh, sm]
        put(stage_n, s * NB, rows)
        if o == 0:
            kh, kl = two_parts(speed)
            zh, zm = two_parts(dot3(c, c))
            none = [zeros, zeros]
            rows = ch * 2 + [-ones, -ones] + cm * 2 + [-ph, -pm] + vh * 2 + none + vl * 2 + none
            put(stage_t, 0, rows)
            rows = twice(vh) * 2 + none + twice(vl) * 2 + [kh, kl]
            rows += [zeros] * 6 + [ones, ones] + [zeros] * 8
            put(stage_t, NB, rows)
            rows = [zeros] * 14 + [zh, zm] + twice(ch) * 2 + none + twice(cm) * 2 + [ones, ones]
            put(stage_t, 2 * NB, rows)
            for b in range(NB):
                for g in range(3):
                    rows_of = pl.ds(33 * (g * NB + b), 32)
                    goal[b, :, g * BLK : (g + 1) * BLK] = stage_t[rows_of, :].astype(BF16)

    for o in (0, 1, 2, 3):
        wait_forces(o)
    for o in (0, 1, 2, 3):
        scatter(o)
    for o in (1, 2, 3):
        node_velocity(o)
    for o in (1, 2):
        gather(o)
    for o in (-1, -2, -3):
        wait_forces(o)
    for o in (-1, -2, -3):
        scatter(o)
    for o in (0, -1, -2):
        node_velocity(o)
    for o in (0, -1, -2):
        gather(o)

    block_rows = lax.broadcasted_iota(jnp.int32, (NB, BLK), 0)

    def some_pairs(n, near):
        pairs = [(cand_t[TOGETHER * n + k], cand_s[TOGETHER * n + k]) for k in range(TOGETHER)]
        dots = []
        for k in range(TOGETHER + SOONER):
            if k < TOGETHER:
                into, source = pairs[k]
                there = jnp.transpose(stage_n[pl.ds(source * 33, 32), :]).astype(BF16)
                dots.append(lax.dot_general(there, goal[into], NN, preferred_element_type=F32))
            if k < SOONER:
                continue
            into, both = pairs[k - SOONER][0], dots[k - SOONER]
            ahead = both[:, 0:BLK]
            square = both[:, BLK : 2 * BLK]
            kept = jnp.minimum(jnp.maximum(ahead, 0.0), square)
            fraction = kept / square
            near_by = jnp.exp(
                fraction * (2.0 * ahead - kept + CORE_SQUARE * fraction) - both[:, 2 * BLK :]
            )
            row = jnp.sum(near_by, axis=0, keepdims=True)
            near = near + jnp.where(block_rows == into, jnp.broadcast_to(row, (NB, BLK)), 0.0)
        return near

    near = lax.fori_loop(0, NCAND // TOGETHER, some_pairs, jnp.zeros((NB, BLK), F32))
    nearness_out[...] = math.exp(CORE_SQUARE) * near

    for copy in sends_b:
        copy.wait_send()


def local(
    centres,
    seg_lines,
    burgers,
    neighbour_blocks,
    seg_nodes,
    node_owner,
    mobility,
    cand_target,
    cand_source,
):
    n_cells = lax.axis_size("cells")
    window = 2 * WIDE + 1
    hbm = pl.BlockSpec(memory_space=pltpu.HBM)
    vmem = pl.BlockSpec(memory_space=pltpu.VMEM)
    velocity, nearness = pl.pallas_call(
        functools.partial(kernel, n_cells),
        name="dislocation_step",
        out_shape=(
            jax.ShapeDtypeStruct((3, SEG), F32),
            jax.ShapeDtypeStruct((NB, BLK), F32),
        ),
        in_specs=[hbm] * 9,
        out_specs=(vmem, vmem),
        scratch_shapes=[
            pltpu.VMEM((3, SEG), F32),
            pltpu.VMEM((3, SEG), F32),
            pltpu.VMEM((3, SEG), F32),
            pltpu.VMEM((2, SEG), jnp.int32),
            pltpu.VMEM((2, SEG), jnp.int32),
            pltpu.VMEM((SPAN, 2, SEG), jnp.int32),
            pltpu.SMEM((NCAND,), jnp.int32),
            pltpu.SMEM((NCAND,), jnp.int32),
            pltpu.VMEM((NB, BLK), F32),
            pltpu.SMEM((NB, NENT), jnp.int32),
            pltpu.VMEM((NB, NENT), jnp.int32),
            pltpu.SMEM((NB, NENT), jnp.int32),
            pltpu.VMEM((window, 72, BLK), F32),
            pltpu.VMEM((window * NB * 49, BLK), F32),
            pltpu.VMEM((window * NB * 17, BLK), F32),
            pltpu.VMEM((NB * 25, BLK), F32),
            pltpu.VMEM((NB * 17, BLK), F32),
            pltpu.VMEM((window * NB * 33, BLK), F32),
            pltpu.VMEM((3 * NB * 33, BLK), F32),
            pltpu.VMEM((window * NB, BLK, 48), BF16),
            pltpu.VMEM((window * NB, 16, 2 * BLK), BF16),
            pltpu.VMEM((NB, 48, 2 * BLK), BF16),
            pltpu.VMEM((NB, 32, 3 * BLK), BF16),
            pltpu.VMEM((SPAN, 2, NB, BLK), jnp.int32),
            pltpu.VMEM((SPAN, BLK, 2 * SEG), BF16),
            pltpu.VMEM((SPAN, 16, 2 * SEG), F32),
            pltpu.VMEM((NB, BLK), F32),
            pltpu.VMEM((NB, BLK), F32),
            pltpu.VMEM((NB, 1, BLK), F32),
            pltpu.VMEM((SPAN, NB, 4, BLK), F32),
            pltpu.VMEM((SPAN, 3, NB, BLK), F32),
            pltpu.SemaphoreType.DMA((9,)),
            pltpu.SemaphoreType.DMA((window,)),
            pltpu.SemaphoreType.DMA((window,)),
            pltpu.SemaphoreType.DMA((SPAN,)),
            pltpu.SemaphoreType.DMA((SPAN,)),
            pltpu.SemaphoreType.DMA((5,)),
            pltpu.SemaphoreType.DMA((SPAN, 2)),
            pltpu.SemaphoreType.DMA((SPAN, 2)),
        ],
        compiler_params=pltpu.CompilerParams(
            collective_id=0, has_side_effects=True, vmem_limit_bytes=60 * 1024 * 1024
        ),
    )(
        neighbour_blocks,
        cand_target,
        cand_source,
        centres,
        seg_lines,
        burgers,
        seg_nodes,
        node_owner,
        mobility.reshape(NB, BLK),
    )
    return velocity, nearness.reshape(SEG)


def solution(mesh):
    in_specs = (
        P(None, "cells"),
        P(None, "cells"),
        P(None, "cells"),
        P("cells", "lanes"),
        P(None, "cells"),
        P(None, "cells"),
        P("cells"),
        P("cells"),
        P("cells"),
    )
    out_specs = (P(None, "cells"), P("cells"))
    return jax.shard_map(local, mesh=mesh, in_specs=in_specs, out_specs=out_specs, check_vma=False)
```

```python
import functools
import math

import jax
import jax.numpy as jnp
from jax import lax
from jax.experimental import pallas as pl
from jax.experimental.pallas import tpu as pltpu
from jax.sharding import PartitionSpec as P

BLK = 128
NB = 8
SEG = BLK * NB
HALF = NB // 2
NENT = 8
NCAND = 32
WIDE = 2
FAR = 3
SPAN = 2 * FAR + 1
FORCE_SCALE = 0.02
CORE_SQUARE = 0.25
TIME_STEP = 4.0
CENTRE = 2.0
TOGETHER = 16
SOONER = 4
AHEAD = 8
ABREAST = 4
F32 = jnp.float32
BF16 = jnp.bfloat16
MESH = pl.DeviceIdType.MESH
NN = (((1,), (0,)), ((), ()))


def rounded(x):
    return x.astype(BF16).astype(F32)


def two_parts(x):
    top = rounded(x)
    return top, rounded(x - top)


def three_parts(x):
    top = rounded(x)
    rest = x - top
    mid = rounded(rest)
    return top, mid, rounded(rest - mid)


def kernel(
    n_cells,
    lists_hbm,
    cand_t_hbm,
    cand_s_hbm,
    centres_hbm,
    lines_hbm,
    burgers_hbm,
    nodes_hbm,
    owner_hbm,
    mobility_hbm,
    velocity_out,
    nearness_out,
    win_c,
    win_l,
    win_b,
    nodes,
    owner,
    codes_r,
    cand_t,
    cand_s,
    mobility,
    list_own,
    list_far_v,
    list_far,
    dense,
    stage_f,
    stage_p,
    stage_q,
    stage_a,
    stage_n,
    stage_t,
    feat,
    pull,
    target,
    goal,
    codes_d,
    onehot,
    mask16,
    drag_send,
    drag_recv,
    eff,
    fbuf,
    vel,
    local_sem,
    send_a,
    recv_a,
    send_n,
    recv_n,
    misc_sem,
    send_b,
    recv_b,
):
    me = lax.axis_index("cells")
    lane = lax.axis_index("lanes")
    other = 1 - lane

    def cell(offset):
        return lax.rem(me + (offset + n_cells), n_cells)

    partners = [
        (o, far) for o in (3, -3, 2, -2, 1, -1, 0) for far in (True, False) if (o, far) != (0, False)
    ]

    greeted = [(o, False) for o in (3, -3, 2, -2, 1, -1)] + [(0, True)]
    barrier = pltpu.get_barrier_semaphore()
    for o, far in greeted:
        pl.semaphore_signal(
            barrier, inc=1, device_id=(cell(o), other if far else lane), device_id_type=MESH
        )
    own_copies = [
        pltpu.make_async_copy(centres_hbm, win_c, local_sem.at[0]),
        pltpu.make_async_copy(lines_hbm, win_l, local_sem.at[1]),
        pltpu.make_async_copy(burgers_hbm, win_b, local_sem.at[2]),
        pltpu.make_async_copy(nodes_hbm, nodes, local_sem.at[3]),
        pltpu.make_async_copy(owner_hbm, owner, local_sem.at[4]),
        pltpu.make_async_copy(lists_hbm, list_own, local_sem.at[5]),
        pltpu.make_async_copy(mobility_hbm, mobility, local_sem.at[6]),
        pltpu.make_async_copy(cand_t_hbm, cand_t, local_sem.at[7]),
        pltpu.make_async_copy(cand_s_hbm, cand_s, local_sem.at[8]),
    ]
    for copy in own_copies:
        copy.start()
    for copy in own_copies:
        copy.wait()

    for a, win in enumerate((win_c, win_l, win_b)):
        for b in range(NB):
            dense[WIDE, pl.ds(24 * a + b, 3, stride=NB), :] = win[:, b * BLK : (b + 1) * BLK]
    codes_r[FAR] = nodes[...] + SEG * owner[...]
    pl.semaphore_wait(barrier, len(greeted))

    def remote(src, dst, send, recv, o, far):
        return pltpu.make_async_remote_copy(
            src_ref=src,
            dst_ref=dst,
            send_sem=send,
            recv_sem=recv,
            device_id=(cell(o), other if far else lane),
            device_id_type=MESH,
        )

    list_copy = remote(lists_hbm, list_far_v, misc_sem.at[0], misc_sem.at[1], 0, True)
    list_copy.start()
    sends_a = {}
    for o in (-2, -1, 2, 1):
        slot = WIDE - o
        sends_a[o] = remote(
            dense.at[WIDE], dense.at[slot], send_a.at[WIDE + o], recv_a.at[slot], o, False
        )
        sends_a[o].start()
    sends_n = {}
    for o in (-3, -2, -1, 3, 2, 1):
        slot = FAR - o
        sends_n[o] = remote(
            codes_r.at[FAR], codes_r.at[slot], send_n.at[FAR + o], recv_n.at[slot], o, False
        )
        sends_n[o].start()

    def build_codes(slot):
        lanes = lax.broadcasted_iota(jnp.int32, (BLK, BLK), 1).astype(F32)
        for e in range(2):
            node = codes_r[slot, e : e + 1, :]
            high = lax.shift_right_logical(node, 7)
            rows16 = lax.broadcasted_iota(jnp.int32, (16, SEG), 0)
            mask16[slot, :, pl.ds(e * SEG, SEG)] = (rows16 == high).astype(F32)
            for b in range(NB):
                codes_d[slot, e, b : b + 1, :] = node[:, b * BLK : (b + 1) * BLK]
            low = jnp.bitwise_and(codes_d[slot, e], BLK - 1).astype(F32)
            turned = jnp.transpose(low)
            for b in range(NB):
                column = jnp.broadcast_to(turned[:, b : b + 1], (BLK, BLK))
                rows = pl.ds(e * SEG + b * BLK, BLK)
                onehot[slot, rows, :] = (column == lanes).astype(F32).astype(BF16)

    ones = jnp.ones((NB, BLK), F32)
    zeros = jnp.zeros((NB, BLK), F32)

    def odd(rows):
        return len(rows) | 1

    def put(ref, base, rows):
        for r, row in enumerate(rows):
            ref[pl.ds(base * odd(rows) + r, NB, stride=odd(rows)), :] = row

    def dense_fields(s):
        parts = [dense[s, NB * k : NB * (k + 1), :] for k in range(9)]
        return [x - CENTRE for x in parts[0:3]], parts[3:6], parts[6:9]

    def dot3(x, y):
        return x[0] * y[0] + x[1] * y[1] + x[2] * y[2]

    def split3(rows):
        return [list(x) for x in zip(*(three_parts(row) for row in rows))]

    def split2(rows):
        return [list(x) for x in zip(*(two_parts(row) for row in rows))]

    def build_source(s):
        c, line, burg = dense_fields(s)
        ch, cm, cl = split3(c)
        sh, sm, sl = three_parts(dot3(c, c) + CORE_SQUARE)
        bh, bm = split2(burg)
        rows = ch + cm + [sh, sm] + ch + cm + [ones, ones] + cl + ch + [sl, ones]
        rows += (bh + bm + [zeros, zeros]) * 2 + [zeros] * 8
        put(stage_f, s * NB, rows)
        moment = [
            line[1] * c[2] - line[2] * c[1],
            line[2] * c[0] - line[0] * c[2],
            line[0] * c[1] - line[1] * c[0],
        ]
        high, low = split2(line + moment)
        put(stage_p, s * NB, high + [zeros, zeros] + low + [zeros, zeros])
        for b in range(s * NB, (s + 1) * NB):
            feat[b] = jnp.transpose(stage_f[49 * b : 49 * b + 48, :]).astype(BF16)
            pulls = stage_p[17 * b : 17 * b + 16, :].astype(BF16)
            pull[b] = jnp.concatenate([pulls, pulls], axis=1)
        return c, line, (ch, cm, cl), (sh, sm)

    centre_own, line_own, (ch, cm, cl), own_square = build_source(WIDE)

    def twice(rows):
        return [-2.0 * row for row in rows]

    zh, zm, zl = three_parts(dot3(centre_own, centre_own))
    lh, lm = split2(line_own)
    rows = twice(ch) * 2 + [ones, ones] + twice(cm) * 2 + [zh, zm]
    rows += twice(ch) + twice(cl) + [ones, zl]
    put(stage_q, 0, rows)
    put(stage_a, 0, lh * 2 + [zeros, zeros] + lm * 2 + [zeros, zeros])
    for b in range(NB):
        right = jnp.concatenate([stage_q[25 * b : 25 * b + 24, :], jnp.zeros((24, BLK), F32)], 0)
        target[b, :, 0:BLK] = right.astype(BF16)
        right = jnp.concatenate(
            [
                jnp.zeros((24, BLK), F32),
                stage_a[17 * b : 17 * b + 16, :],
                jnp.zeros((8, BLK), F32),
            ],
            0,
        )
        target[b, :, BLK : 2 * BLK] = right.astype(BF16)

    build_codes(FAR)
    line = [win_l[k : k + 1, :] for k in range(3)]
    length = 0.5 * jnp.sqrt(dot3(line, line))
    drag = jnp.zeros((32, BLK), F32)
    for e in range(2):
        span = slice(e * SEG, (e + 1) * SEG)
        mask = mask16[FAR, :, span] > 0.5
        parts = [
            jnp.where(mask, jnp.broadcast_to(part, (16, SEG)), 0.0) for part in two_parts(length)
        ]
        drag = drag + lax.dot_general(
            jnp.concatenate(parts, axis=0).astype(BF16),
            onehot[FAR, span, :],
            NN,
            preferred_element_type=F32,
        )
    drag_send[...] = drag[8:16] + drag[24:32]
    drag_copy = remote(drag_send, drag_recv, misc_sem.at[2], misc_sem.at[3], 1, False)
    drag_copy.start()
    own_drag = drag[0:8] + drag[16:24]

    kept_centres = {0: (centre_own, line_own, (ch, cm, cl), own_square)}
    for o in (1, -1, 2, -2):
        sends_a[-o].wait_recv()
        kept_centres[o] = build_source(WIDE + o)
    list_copy.wait_recv()
    to_smem = pltpu.make_async_copy(list_far_v, list_far, misc_sem.at[4])
    to_smem.start()
    to_smem.wait()
    drag_copy.wait_recv()
    eff_all = mobility[...] / (1.0 + (own_drag + drag_recv[...]))
    for b in range(NB):
        eff[b] = eff_all[b : b + 1, :]

    def some_targets(t, carry):
        blocks = [HALF * lane + t * ABREAST + k for k in range(ABREAST)]
        rights = [target[block] for block in blocks]
        totals = [jnp.zeros((16, BLK), F32) for block in blocks]
        sources = [
            (k, lists[block, e])
            for k, block in enumerate(blocks)
            for lists in (list_own, list_far)
            for e in range(NENT)
        ]
        ahead = []
        for n in range(len(sources) + AHEAD):
            if n < len(sources):
                k, source = sources[n]
                ahead.append(
                    lax.dot_general(feat[source], rights[k], NN, preferred_element_type=F32)
                )
            if n < AHEAD:
                continue
            both = ahead[n - AHEAD]
            inverse = lax.rsqrt(both[:, 0:BLK])
            weight = both[:, BLK : 2 * BLK] * inverse * inverse * inverse
            top = weight.astype(BF16)
            low = (weight - top.astype(F32)).astype(BF16)
            k, source = sources[n - AHEAD]
            totals[k] = totals[k] + lax.dot_general(
                pull[source],
                jnp.concatenate([top, low], axis=0),
                NN,
                preferred_element_type=F32,
            )
        for block, total in zip(blocks, totals):
            total = total[0:8] + total[8:16]
            cut = pl.ds(pl.multiple_of(block * BLK, BLK), BLK)
            x, y, z = (win_c[k : k + 1, cut] - CENTRE for k in range(3))
            sx, sy, sz = (total[k : k + 1] for k in range(3))
            scale = 0.5 * FORCE_SCALE
            fbuf[FAR, block, 0:1, :] = scale * (sy * z - sz * y - total[3:4])
            fbuf[FAR, block, 1:2, :] = scale * (sz * x - sx * z - total[4:5])
            fbuf[FAR, block, 2:3, :] = scale * (sx * y - sy * x - total[5:6])
            fbuf[FAR, block, 3:4, :] = eff[block]
        return carry

    lax.fori_loop(0, HALF // ABREAST, some_targets, 0)

    for copy in sends_n.values():
        copy.wait_recv()

    mine = pl.ds(HALF * lane, HALF)
    sends_b = []
    for o, far in partners:
        slot = FAR - o
        copy = remote(
            fbuf.at[FAR, mine],
            fbuf.at[slot, mine],
            send_b.at[FAR + o, int(far)],
            recv_b.at[slot, int(far)],
            o,
            far,
        )
        copy.start()
        sends_b.append(copy)

    for o in (1, -1, 2, -2, 3, -3):
        build_codes(FAR + o)
    for copy in list(sends_a.values()) + list(sends_n.values()) + [list_copy, drag_copy]:
        copy.wait_send()

    own_part = {}
    next_part = {}
    recv_of = dict(zip(partners, sends_b))

    def wait_forces(o):
        for far in (False, True):
            if (-o, far) in recv_of:
                recv_of[(-o, far)].wait_recv()

    def scatter(o):
        slot = FAR + o
        forces = jnp.concatenate([fbuf[slot, b] for b in range(NB)], axis=1)
        parts = two_parts(forces)
        first = NB if o == -FAR else 0
        last = NB if o == FAR else 2 * NB
        size = last - first
        total = jnp.zeros((6 * size, BLK), F32)
        for e in range(2):
            span = slice(e * SEG, (e + 1) * SEG)
            mask = mask16[slot, first:last, span] > 0.5
            stack = [
                jnp.where(mask, jnp.broadcast_to(part[k : k + 1], (size, SEG)), 0.0)
                for part in parts
                for k in range(3)
            ]
            total = total + lax.dot_general(
                jnp.concatenate(stack, axis=0).astype(BF16),
                onehot[slot, span, :],
                NN,
                preferred_element_type=F32,
            )
        total = total[0 : 3 * size] + total[3 * size : 6 * size]
        if o < FAR:
            next_part[o] = [total[size * (k + 1) - NB : size * (k + 1)] for k in range(3)]
        if o > -FAR:
            own_part[o] = [total[size * k : size * k + NB] for k in range(3)]

    def node_velocity(o):
        eff_o = jnp.concatenate([fbuf[FAR + o, b, 3:4, :] for b in range(NB)], axis=0)
        for k in range(3):
            value = eff_o * (own_part[o][k] + next_part[o - 1][k])
            vel[FAR + o, k] = value
            if o == 0:
                for b in range(NB):
                    velocity_out[k : k + 1, b * BLK : (b + 1) * BLK] = value[b : b + 1, :]

    shift = []

    def gather(o):
        slot = FAR + o
        s = WIDE + o
        moved = [zeros, zeros, zeros]
        for e in range(2):
            code = codes_d[slot, e]
            low = jnp.bitwise_and(code, BLK - 1)
            high = lax.shift_right_logical(code, 7)
            picked = [zeros, zeros, zeros]
            for h in range(16):
                here = high == h
                for k in range(3):
                    row = vel[slot + h // NB, k, h % NB : h % NB + 1, :]
                    table = jnp.broadcast_to(row, (NB, BLK))
                    found = jnp.take_along_axis(table, low, axis=1, mode="promise_in_bounds")
                    picked[k] = jnp.where(here, found, picked[k])
            moved = [x + y for x, y in zip(moved, picked)]
        moved = [0.5 * TIME_STEP * x for x in moved]
        if not shift:
            shift.extend(
                jnp.sum(jnp.sum(x, axis=1, keepdims=True), axis=0, keepdims=True) / SEG
                for x in moved
            )
        moved = [x - jnp.broadcast_to(y, (NB, BLK)) for x, y in zip(moved, shift)]
        c, unused, (ch, cm, cl), (sh, sm) = kept_centres[o]
        vh, vl = split2(moved)
        ph, pm = two_parts(dot3(c, moved))
        speed = dot3(moved, moved)
        mh, ml = two_parts(speed + CORE_SQUARE)
        rows = vh + vl + [ph, pm] + vh + vl + [ones, ones]
        rows += ch + cm + [mh, ml] + ch + cm + [sh, sm]
        put(stage_n, s * NB, rows)
        if o == 0:
            kh, kl = two_parts(speed)
            zh, zm = two_parts(dot3(c, c))
            none = [zeros, zeros]
            rows = ch * 2 + [-ones, -ones] + cm * 2 + [-ph, -pm] + vh * 2 + none + vl * 2 + none
            put(stage_t, 0, rows)
            rows = twice(vh) * 2 + none + twice(vl) * 2 + [kh, kl]
            rows += [zeros] * 6 + [ones, ones] + [zeros] * 8
            put(stage_t, NB, rows)
            rows = [zeros] * 14 + [zh, zm] + twice(ch) * 2 + none + twice(cm) * 2 + [ones, ones]
            put(stage_t, 2 * NB, rows)
            for b in range(NB):
                for g in range(3):
                    rows_of = pl.ds(33 * (g * NB + b), 32)
                    goal[b, :, g * BLK : (g + 1) * BLK] = stage_t[rows_of, :].astype(BF16)

    for o in (0, 1, 2, 3):
        wait_forces(o)
    for o in (0, 1, 2, 3):
        scatter(o)
    for o in (1, 2, 3):
        node_velocity(o)
    for o in (1, 2):
        gather(o)
    for o in (-1, -2, -3):
        wait_forces(o)
    for o in (-1, -2, -3):
        scatter(o)
    for o in (0, -1, -2):
        node_velocity(o)
    for o in (0, -1, -2):
        gather(o)

    block_rows = lax.broadcasted_iota(jnp.int32, (NB, BLK), 0)

    def some_pairs(n, near):
        pairs = [(cand_t[TOGETHER * n + k], cand_s[TOGETHER * n + k]) for k in range(TOGETHER)]
        dots = []
        for k in range(TOGETHER + SOONER):
            if k < TOGETHER:
                into, source = pairs[k]
                there = jnp.transpose(stage_n[pl.ds(source * 33, 32), :]).astype(BF16)
                dots.append(lax.dot_general(there, goal[into], NN, preferred_element_type=F32))
            if k < SOONER:
                continue
            into, both = pairs[k - SOONER][0], dots[k - SOONER]
            ahead = both[:, 0:BLK]
            square = both[:, BLK : 2 * BLK]
            kept = jnp.minimum(jnp.maximum(ahead, 0.0), square)
            fraction = kept / square
            near_by = jnp.exp(
                fraction * (2.0 * ahead - kept + CORE_SQUARE * fraction) - both[:, 2 * BLK :]
            )
            row = jnp.sum(near_by, axis=0, keepdims=True)
            near = near + jnp.where(block_rows == into, jnp.broadcast_to(row, (NB, BLK)), 0.0)
        return near

    near = lax.fori_loop(0, NCAND // TOGETHER, some_pairs, jnp.zeros((NB, BLK), F32))
    nearness_out[...] = math.exp(CORE_SQUARE) * near

    for copy in sends_b:
        copy.wait_send()


def local(
    centres,
    seg_lines,
    burgers,
    neighbour_blocks,
    seg_nodes,
    node_owner,
    mobility,
    cand_target,
    cand_source,
):
    n_cells = lax.axis_size("cells")
    window = 2 * WIDE + 1
    hbm = pl.BlockSpec(memory_space=pltpu.HBM)
    vmem = pl.BlockSpec(memory_space=pltpu.VMEM)
    velocity, nearness = pl.pallas_call(
        functools.partial(kernel, n_cells),
        name="dislocation_step",
        out_shape=(
            pltpu.VMEM((3, SEG), F32),
            pltpu.VMEM((NB, BLK), F32),
        ),
        in_specs=[hbm] * 9,
        out_specs=(vmem, vmem),
        scratch_shapes=[
            pltpu.VMEM((3, SEG), F32),
            pltpu.VMEM((3, SEG), F32),
            pltpu.VMEM((3, SEG), F32),
            pltpu.VMEM((2, SEG), jnp.int32),
            pltpu.VMEM((2, SEG), jnp.int32),
            pltpu.VMEM((SPAN, 2, SEG), jnp.int32),
            pltpu.SMEM((NCAND,), jnp.int32),
            pltpu.SMEM((NCAND,), jnp.int32),
            pltpu.VMEM((NB, BLK), F32),
            pltpu.SMEM((NB, NENT), jnp.int32),
            pltpu.VMEM((NB, NENT), jnp.int32),
            pltpu.SMEM((NB, NENT), jnp.int32),
            pltpu.VMEM((window, 72, BLK), F32),
            pltpu.VMEM((window * NB * 49, BLK), F32),
            pltpu.VMEM((window * NB * 17, BLK), F32),
            pltpu.VMEM((NB * 25, BLK), F32),
            pltpu.VMEM((NB * 17, BLK), F32),
            pltpu.VMEM((window * NB * 33, BLK), F32),
            pltpu.VMEM((3 * NB * 33, BLK), F32),
            pltpu.VMEM((window * NB, BLK, 48), BF16),
            pltpu.VMEM((window * NB, 16, 2 * BLK), BF16),
            pltpu.VMEM((NB, 48, 2 * BLK), BF16),
            pltpu.VMEM((NB, 32, 3 * BLK), BF16),
            pltpu.VMEM((SPAN, 2, NB, BLK), jnp.int32),
            pltpu.VMEM((SPAN, 2 * SEG, BLK), BF16),
            pltpu.VMEM((SPAN, 16, 2 * SEG), F32),
            pltpu.VMEM((NB, BLK), F32),
            pltpu.VMEM((NB, BLK), F32),
            pltpu.VMEM((NB, 1, BLK), F32),
            pltpu.VMEM((SPAN, NB, 4, BLK), F32),
            pltpu.VMEM((SPAN, 3, NB, BLK), F32),
            pltpu.SemaphoreType.DMA((9,)),
            pltpu.SemaphoreType.DMA((window,)),
            pltpu.SemaphoreType.DMA((window,)),
            pltpu.SemaphoreType.DMA((SPAN,)),
            pltpu.SemaphoreType.DMA((SPAN,)),
            pltpu.SemaphoreType.DMA((5,)),
            pltpu.SemaphoreType.DMA((SPAN, 2)),
            pltpu.SemaphoreType.DMA((SPAN, 2)),
        ],
        compiler_params=pltpu.CompilerParams(
            collective_id=0, has_side_effects=True, vmem_limit_bytes=60 * 1024 * 1024
        ),
    )(
        neighbour_blocks,
        cand_target,
        cand_source,
        centres,
        seg_lines,
        burgers,
        seg_nodes,
        node_owner,
        mobility.reshape(NB, BLK),
    )
    return velocity, nearness.reshape(SEG)


def solution(mesh):
    in_specs = (
        P(None, "cells"),
        P(None, "cells"),
        P(None, "cells"),
        P("cells", "lanes"),
        P(None, "cells"),
        P(None, "cells"),
        P("cells"),
        P("cells"),
        P("cells"),
    )
    out_specs = (P(None, "cells"), P("cells"))
    return jax.shard_map(local, mesh=mesh, in_specs=in_specs, out_specs=out_specs, check_vma=False)
```

```python
import functools
import math

import jax
import jax.numpy as jnp
from jax import lax
from jax.experimental import pallas as pl
from jax.experimental.pallas import tpu as pltpu
from jax.sharding import PartitionSpec as P

BLK = 128
NB = 8
SEG = BLK * NB
HALF = NB // 2
NENT = 8
NCAND = 32
WIDE = 2
FAR = 3
SPAN = 2 * FAR + 1
FORCE_SCALE = 0.02
CORE_SQUARE = 0.25
TIME_STEP = 4.0
CENTRE = 2.0
TOGETHER = 16
SOONER = 4
AHEAD = 8
ABREAST = 4
F32 = jnp.float32
BF16 = jnp.bfloat16
MESH = pl.DeviceIdType.MESH
NN = (((1,), (0,)), ((), ()))


def rounded(x):
    return x.astype(BF16).astype(F32)


def two_parts(x):
    top = rounded(x)
    return top, rounded(x - top)


def three_parts(x):
    top = rounded(x)
    rest = x - top
    mid = rounded(rest)
    return top, mid, rounded(rest - mid)


def kernel(
    n_cells,
    lists_hbm,
    cand_t_hbm,
    cand_s_hbm,
    centres_hbm,
    lines_hbm,
    burgers_hbm,
    nodes_hbm,
    owner_hbm,
    mobility_hbm,
    velocity_out,
    nearness_out,
    win_c,
    win_l,
    win_b,
    nodes,
    owner,
    codes_r,
    cand_t,
    cand_s,
    mobility,
    list_own,
    list_far_v,
    list_far,
    dense,
    stage_f,
    stage_p,
    stage_q,
    stage_a,
    stage_n,
    stage_t,
    feat,
    pull,
    target,
    goal,
    codes_d,
    onehot,
    mask16,
    drag_send,
    drag_recv,
    eff,
    fbuf,
    vel,
    local_sem,
    send_a,
    recv_a,
    send_n,
    recv_n,
    misc_sem,
    send_b,
    recv_b,
):
    me = lax.axis_index("cells")
    lane = lax.axis_index("lanes")
    other = 1 - lane

    def cell(offset):
        return lax.rem(me + (offset + n_cells), n_cells)

    partners = [
        (o, far) for o in (3, -3, 2, -2, 1, -1, 0) for far in (True, False) if (o, far) != (0, False)
    ]

    greeted = [(o, False) for o in (3, -3, 2, -2, 1, -1)] + [(0, True)]
    barrier = pltpu.get_barrier_semaphore()
    for o, far in greeted:
        pl.semaphore_signal(
            barrier, inc=1, device_id=(cell(o), other if far else lane), device_id_type=MESH
        )
    own_copies = [
        pltpu.make_async_copy(centres_hbm, win_c, local_sem.at[0]),
        pltpu.make_async_copy(lines_hbm, win_l, local_sem.at[1]),
        pltpu.make_async_copy(burgers_hbm, win_b, local_sem.at[2]),
        pltpu.make_async_copy(nodes_hbm, nodes, local_sem.at[3]),
        pltpu.make_async_copy(owner_hbm, owner, local_sem.at[4]),
        pltpu.make_async_copy(lists_hbm, list_own, local_sem.at[5]),
        pltpu.make_async_copy(mobility_hbm, mobility, local_sem.at[6]),
        pltpu.make_async_copy(cand_t_hbm, cand_t, local_sem.at[7]),
        pltpu.make_async_copy(cand_s_hbm, cand_s, local_sem.at[8]),
    ]
    for copy in own_copies:
        copy.start()
    for copy in own_copies:
        copy.wait()

    for a, win in enumerate((win_c, win_l, win_b)):
        for b in range(NB):
            dense[WIDE, pl.ds(24 * a + b, 3, stride=NB), :] = win[:, b * BLK : (b + 1) * BLK]
    codes_r[FAR] = nodes[...] + SEG * owner[...]
    pl.semaphore_wait(barrier, len(greeted))

    def remote(src, dst, send, recv, o, far):
        return pltpu.make_async_remote_copy(
            src_ref=src,
            dst_ref=dst,
            send_sem=send,
            recv_sem=recv,
            device_id=(cell(o), other if far else lane),
            device_id_type=MESH,
        )

    list_copy = remote(lists_hbm, list_far_v, misc_sem.at[0], misc_sem.at[1], 0, True)
    list_copy.start()
    sends_a = {}
    for o in (-2, -1, 2, 1):
        slot = WIDE - o
        sends_a[o] = remote(
            dense.at[WIDE], dense.at[slot], send_a.at[WIDE + o], recv_a.at[slot], o, False
        )
        sends_a[o].start()
    sends_n = {}
    for o in (-3, -2, -1, 3, 2, 1):
        slot = FAR - o
        sends_n[o] = remote(
            codes_r.at[FAR], codes_r.at[slot], send_n.at[FAR + o], recv_n.at[slot], o, False
        )
        sends_n[o].start()

    def build_codes(slot):
        lanes = lax.broadcasted_iota(jnp.int32, (BLK, BLK), 1).astype(F32)
        for e in range(2):
            node = codes_r[slot, e : e + 1, :]
            high = lax.shift_right_logical(node, 7)
            rows16 = lax.broadcasted_iota(jnp.int32, (16, SEG), 0)
            mask16[slot, :, pl.ds(e * SEG, SEG)] = (rows16 == high).astype(F32)
            for b in range(NB):
                codes_d[slot, e, b : b + 1, :] = node[:, b * BLK : (b + 1) * BLK]
            low = jnp.bitwise_and(codes_d[slot, e], BLK - 1).astype(F32)
            turned = jnp.transpose(low)
            for b in range(NB):
                column = jnp.broadcast_to(turned[:, b : b + 1], (BLK, BLK))
                rows = pl.ds(e * SEG + b * BLK, BLK)
                onehot[slot, rows, :] = (column == lanes).astype(F32).astype(BF16)

    ones = jnp.ones((NB, BLK), F32)
    zeros = jnp.zeros((NB, BLK), F32)

    def odd(rows):
        return len(rows) | 1

    def put(ref, base, rows):
        for r, row in enumerate(rows):
            ref[pl.ds(base * odd(rows) + r, NB, stride=odd(rows)), :] = row

    def dense_fields(s):
        parts = [dense[s, NB * k : NB * (k + 1), :] for k in range(9)]
        return [x - CENTRE for x in parts[0:3]], parts[3:6], parts[6:9]

    def dot3(x, y):
        return x[0] * y[0] + x[1] * y[1] + x[2] * y[2]

    def split3(rows):
        return [list(x) for x in zip(*(three_parts(row) for row in rows))]

    def split2(rows):
        return [list(x) for x in zip(*(two_parts(row) for row in rows))]

    def build_source(s):
        c, line, burg = dense_fields(s)
        ch, cm, cl = split3(c)
        sh, sm, sl = three_parts(dot3(c, c) + CORE_SQUARE)
        bh, bm = split2(burg)
        rows = ch + cm + [sh, sm] + ch + cm + [ones, ones] + cl + ch + [sl, ones]
        rows += (bh + bm + [zeros, zeros]) * 2 + [zeros] * 8
        put(stage_f, s * NB, rows)
        moment = [
            line[1] * c[2] - line[2] * c[1],
            line[2] * c[0] - line[0] * c[2],
            line[0] * c[1] - line[1] * c[0],
        ]
        high, low = split2(line + moment)
        put(stage_p, s * NB, high + [zeros, zeros] + low + [zeros, zeros])
        for b in range(s * NB, (s + 1) * NB):
            feat[b] = jnp.transpose(stage_f[49 * b : 49 * b + 48, :]).astype(BF16)
            pulls = stage_p[17 * b : 17 * b + 16, :].astype(BF16)
            pull[b] = jnp.concatenate([pulls, pulls], axis=1)
        return c, line, (ch, cm, cl), (sh, sm)

    centre_own, line_own, (ch, cm, cl), own_square = build_source(WIDE)

    def twice(rows):
        return [-2.0 * row for row in rows]

    zh, zm, zl = three_parts(dot3(centre_own, centre_own))
    lh, lm = split2(line_own)
    rows = twice(ch) * 2 + [ones, ones] + twice(cm) * 2 + [zh, zm]
    rows += twice(ch) + twice(cl) + [ones, zl]
    put(stage_q, 0, rows)
    put(stage_a, 0, lh * 2 + [zeros, zeros] + lm * 2 + [zeros, zeros])
    for b in range(NB):
        right = jnp.concatenate([stage_q[25 * b : 25 * b + 24, :], jnp.zeros((24, BLK), F32)], 0)
        target[b, :, 0:BLK] = right.astype(BF16)
        right = jnp.concatenate(
            [
                jnp.zeros((24, BLK), F32),
                stage_a[17 * b : 17 * b + 16, :],
                jnp.zeros((8, BLK), F32),
            ],
            0,
        )
        target[b, :, BLK : 2 * BLK] = right.astype(BF16)

    build_codes(FAR)
    line = [win_l[k : k + 1, :] for k in range(3)]
    length = 0.5 * jnp.sqrt(dot3(line, line))
    drag = jnp.zeros((32, BLK), F32)
    for e in range(2):
        span = slice(e * SEG, (e + 1) * SEG)
        mask = mask16[FAR, :, span] > 0.5
        parts = [
            jnp.where(mask, jnp.broadcast_to(part, (16, SEG)), 0.0) for part in two_parts(length)
        ]
        drag = drag + lax.dot_general(
            jnp.concatenate(parts, axis=0).astype(BF16),
            onehot[FAR, span, :],
            NN,
            preferred_element_type=F32,
        )
    drag_send[...] = drag[8:16] + drag[24:32]
    drag_copy = remote(drag_send, drag_recv, misc_sem.at[2], misc_sem.at[3], 1, False)
    drag_copy.start()
    own_drag = drag[0:8] + drag[16:24]

    kept_centres = {0: (centre_own, line_own, (ch, cm, cl), own_square)}

    def sources_of(pair):
        for o in pair:
            sends_a[-o].wait_recv()
        for o in pair:
            kept_centres[o] = build_source(WIDE + o)

    sources_of((-1, -2))
    list_copy.wait_recv()
    to_smem = pltpu.make_async_copy(list_far_v, list_far, misc_sem.at[4])
    to_smem.start()
    to_smem.wait()
    drag_copy.wait_recv()
    eff_all = mobility[...] / (1.0 + (own_drag + drag_recv[...]))
    for b in range(NB):
        eff[b] = eff_all[b : b + 1, :]
    sources_of((1, 2))

    def some_targets(t, carry):
        blocks = [HALF * lane + t * ABREAST + k for k in range(ABREAST)]
        rights = [target[block] for block in blocks]
        totals = [jnp.zeros((16, BLK), F32) for block in blocks]
        sources = [
            (k, lists[block, e])
            for k, block in enumerate(blocks)
            for lists in (list_own, list_far)
            for e in range(NENT)
        ]
        ahead = []
        for n in range(len(sources) + AHEAD):
            if n < len(sources):
                k, source = sources[n]
                ahead.append(
                    lax.dot_general(feat[source], rights[k], NN, preferred_element_type=F32)
                )
            if n < AHEAD:
                continue
            both = ahead[n - AHEAD]
            inverse = lax.rsqrt(both[:, 0:BLK])
            weight = both[:, BLK : 2 * BLK] * inverse * inverse * inverse
            top = weight.astype(BF16)
            low = (weight - top.astype(F32)).astype(BF16)
            k, source = sources[n - AHEAD]
            totals[k] = totals[k] + lax.dot_general(
                pull[source],
                jnp.concatenate([top, low], axis=0),
                NN,
                preferred_element_type=F32,
            )
        for block, total in zip(blocks, totals):
            total = total[0:8] + total[8:16]
            cut = pl.ds(pl.multiple_of(block * BLK, BLK), BLK)
            x, y, z = (win_c[k : k + 1, cut] - CENTRE for k in range(3))
            sx, sy, sz = (total[k : k + 1] for k in range(3))
            scale = 0.5 * FORCE_SCALE
            fbuf[FAR, block, 0:1, :] = scale * (sy * z - sz * y - total[3:4])
            fbuf[FAR, block, 1:2, :] = scale * (sz * x - sx * z - total[4:5])
            fbuf[FAR, block, 2:3, :] = scale * (sx * y - sy * x - total[5:6])
            fbuf[FAR, block, 3:4, :] = eff[block]
        return carry

    lax.fori_loop(0, HALF // ABREAST, some_targets, 0)

    for copy in sends_n.values():
        copy.wait_recv()

    mine = pl.ds(HALF * lane, HALF)
    sends_b = []
    for o, far in partners:
        slot = FAR - o
        copy = remote(
            fbuf.at[FAR, mine],
            fbuf.at[slot, mine],
            send_b.at[FAR + o, int(far)],
            recv_b.at[slot, int(far)],
            o,
            far,
        )
        copy.start()
        sends_b.append(copy)

    for o in (1, -1, 2, -2, 3, -3):
        build_codes(FAR + o)
    for copy in list(sends_a.values()) + list(sends_n.values()) + [list_copy, drag_copy]:
        copy.wait_send()

    own_part = {}
    next_part = {}
    recv_of = dict(zip(partners, sends_b))

    def wait_forces(o):
        for far in (False, True):
            if (-o, far) in recv_of:
                recv_of[(-o, far)].wait_recv()

    def scatter(o):
        slot = FAR + o
        forces = jnp.concatenate([fbuf[slot, b] for b in range(NB)], axis=1)
        parts = two_parts(forces)
        first = NB if o == -FAR else 0
        last = NB if o == FAR else 2 * NB
        size = last - first
        total = jnp.zeros((6 * size, BLK), F32)
        for e in range(2):
            span = slice(e * SEG, (e + 1) * SEG)
            mask = mask16[slot, first:last, span] > 0.5
            stack = [
                jnp.where(mask, jnp.broadcast_to(part[k : k + 1], (size, SEG)), 0.0)
                for part in parts
                for k in range(3)
            ]
            total = total + lax.dot_general(
                jnp.concatenate(stack, axis=0).astype(BF16),
                onehot[slot, span, :],
                NN,
                preferred_element_type=F32,
            )
        total = total[0 : 3 * size] + total[3 * size : 6 * size]
        if o < FAR:
            next_part[o] = [total[size * (k + 1) - NB : size * (k + 1)] for k in range(3)]
        if o > -FAR:
            own_part[o] = [total[size * k : size * k + NB] for k in range(3)]

    def node_velocity(o):
        eff_o = jnp.concatenate([fbuf[FAR + o, b, 3:4, :] for b in range(NB)], axis=0)
        for k in range(3):
            value = eff_o * (own_part[o][k] + next_part[o - 1][k])
            vel[FAR + o, k] = value
            if o == 0:
                for b in range(NB):
                    velocity_out[k : k + 1, b * BLK : (b + 1) * BLK] = value[b : b + 1, :]

    shift = []

    def gather(o):
        slot = FAR + o
        s = WIDE + o
        moved = [zeros, zeros, zeros]
        for e in range(2):
            code = codes_d[slot, e]
            low = jnp.bitwise_and(code, BLK - 1)
            high = lax.shift_right_logical(code, 7)
            picked = [zeros, zeros, zeros]
            for h in range(16):
                here = high == h
                for k in range(3):
                    row = vel[slot + h // NB, k, h % NB : h % NB + 1, :]
                    table = jnp.broadcast_to(row, (NB, BLK))
                    found = jnp.take_along_axis(table, low, axis=1, mode="promise_in_bounds")
                    picked[k] = jnp.where(here, found, picked[k])
            moved = [x + y for x, y in zip(moved, picked)]
        moved = [0.5 * TIME_STEP * x for x in moved]
        if not shift:
            shift.extend(
                jnp.sum(jnp.sum(x, axis=1, keepdims=True), axis=0, keepdims=True) / SEG
                for x in moved
            )
        moved = [x - jnp.broadcast_to(y, (NB, BLK)) for x, y in zip(moved, shift)]
        c, unused, (ch, cm, cl), (sh, sm) = kept_centres[o]
        vh, vl = split2(moved)
        ph, pm = two_parts(dot3(c, moved))
        speed = dot3(moved, moved)
        mh, ml = two_parts(speed + CORE_SQUARE)
        rows = vh + vl + [ph, pm] + vh + vl + [ones, ones]
        rows += ch + cm + [mh, ml] + ch + cm + [sh, sm]
        put(stage_n, s * NB, rows)
        if o == 0:
            kh, kl = two_parts(speed)
            zh, zm = two_parts(dot3(c, c))
            none = [zeros, zeros]
            rows = ch * 2 + [-ones, -ones] + cm * 2 + [-ph, -pm] + vh * 2 + none + vl * 2 + none
            put(stage_t, 0, rows)
            rows = twice(vh) * 2 + none + twice(vl) * 2 + [kh, kl]
            rows += [zeros] * 6 + [ones, ones] + [zeros] * 8
            put(stage_t, NB, rows)
            rows = [zeros] * 14 + [zh, zm] + twice(ch) * 2 + none + twice(cm) * 2 + [ones, ones]
            put(stage_t, 2 * NB, rows)
            for b in range(NB):
                for g in range(3):
                    rows_of = pl.ds(33 * (g * NB + b), 32)
                    goal[b, :, g * BLK : (g + 1) * BLK] = stage_t[rows_of, :].astype(BF16)

    for o in (0, 1, 2, 3):
        wait_forces(o)
    for o in (0, 1, 2, 3):
        scatter(o)
    for o in (1, 2, 3):
        node_velocity(o)
    for o in (1, 2):
        gather(o)
    for o in (-1, -2, -3):
        wait_forces(o)
    for o in (-1, -2, -3):
        scatter(o)
    for o in (0, -1, -2):
        node_velocity(o)
    for o in (0, -1, -2):
        gather(o)

    block_rows = lax.broadcasted_iota(jnp.int32, (NB, BLK), 0)

    def some_pairs(n, near):
        pairs = [(cand_t[TOGETHER * n + k], cand_s[TOGETHER * n + k]) for k in range(TOGETHER)]
        dots = []
        for k in range(TOGETHER + SOONER):
            if k < TOGETHER:
                into, source = pairs[k]
                there = jnp.transpose(stage_n[pl.ds(source * 33, 32), :]).astype(BF16)
                dots.append(lax.dot_general(there, goal[into], NN, preferred_element_type=F32))
            if k < SOONER:
                continue
            into, both = pairs[k - SOONER][0], dots[k - SOONER]
            ahead = both[:, 0:BLK]
            square = both[:, BLK : 2 * BLK]
            kept = jnp.minimum(jnp.maximum(ahead, 0.0), square)
            fraction = kept / square
            near_by = jnp.exp(
                fraction * (2.0 * ahead - kept + CORE_SQUARE * fraction) - both[:, 2 * BLK :]
            )
            row = jnp.sum(near_by, axis=0, keepdims=True)
            near = near + jnp.where(block_rows == into, jnp.broadcast_to(row, (NB, BLK)), 0.0)
        return near

    near = lax.fori_loop(0, NCAND // TOGETHER, some_pairs, jnp.zeros((NB, BLK), F32))
    nearness_out[...] = math.exp(CORE_SQUARE) * near

    for copy in sends_b:
        copy.wait_send()


def local(
    centres,
    seg_lines,
    burgers,
    neighbour_blocks,
    seg_nodes,
    node_owner,
    mobility,
    cand_target,
    cand_source,
):
    n_cells = lax.axis_size("cells")
    window = 2 * WIDE + 1
    hbm = pl.BlockSpec(memory_space=pltpu.HBM)
    vmem = pl.BlockSpec(memory_space=pltpu.VMEM)
    velocity, nearness = pl.pallas_call(
        functools.partial(kernel, n_cells),
        name="dislocation_step",
        out_shape=(
            pltpu.VMEM((3, SEG), F32),
            pltpu.VMEM((NB, BLK), F32),
        ),
        in_specs=[hbm] * 9,
        out_specs=(vmem, vmem),
        scratch_shapes=[
            pltpu.VMEM((3, SEG), F32),
            pltpu.VMEM((3, SEG), F32),
            pltpu.VMEM((3, SEG), F32),
            pltpu.VMEM((2, SEG), jnp.int32),
            pltpu.VMEM((2, SEG), jnp.int32),
            pltpu.VMEM((SPAN, 2, SEG), jnp.int32),
            pltpu.SMEM((NCAND,), jnp.int32),
            pltpu.SMEM((NCAND,), jnp.int32),
            pltpu.VMEM((NB, BLK), F32),
            pltpu.SMEM((NB, NENT), jnp.int32),
            pltpu.VMEM((NB, NENT), jnp.int32),
            pltpu.SMEM((NB, NENT), jnp.int32),
            pltpu.VMEM((window, 72, BLK), F32),
            pltpu.VMEM((window * NB * 49, BLK), F32),
            pltpu.VMEM((window * NB * 17, BLK), F32),
            pltpu.VMEM((NB * 25, BLK), F32),
            pltpu.VMEM((NB * 17, BLK), F32),
            pltpu.VMEM((window * NB * 33, BLK), F32),
            pltpu.VMEM((3 * NB * 33, BLK), F32),
            pltpu.VMEM((window * NB, BLK, 48), BF16),
            pltpu.VMEM((window * NB, 16, 2 * BLK), BF16),
            pltpu.VMEM((NB, 48, 2 * BLK), BF16),
            pltpu.VMEM((NB, 32, 3 * BLK), BF16),
            pltpu.VMEM((SPAN, 2, NB, BLK), jnp.int32),
            pltpu.VMEM((SPAN, 2 * SEG, BLK), BF16),
            pltpu.VMEM((SPAN, 16, 2 * SEG), F32),
            pltpu.VMEM((NB, BLK), F32),
            pltpu.VMEM((NB, BLK), F32),
            pltpu.VMEM((NB, 1, BLK), F32),
            pltpu.VMEM((SPAN, NB, 4, BLK), F32),
            pltpu.VMEM((SPAN, 3, NB, BLK), F32),
            pltpu.SemaphoreType.DMA((9,)),
            pltpu.SemaphoreType.DMA((window,)),
            pltpu.SemaphoreType.DMA((window,)),
            pltpu.SemaphoreType.DMA((SPAN,)),
            pltpu.SemaphoreType.DMA((SPAN,)),
            pltpu.SemaphoreType.DMA((5,)),
            pltpu.SemaphoreType.DMA((SPAN, 2)),
            pltpu.SemaphoreType.DMA((SPAN, 2)),
        ],
        compiler_params=pltpu.CompilerParams(
            collective_id=0, has_side_effects=True, vmem_limit_bytes=60 * 1024 * 1024
        ),
    )(
        neighbour_blocks,
        cand_target,
        cand_source,
        centres,
        seg_lines,
        burgers,
        seg_nodes,
        node_owner,
        mobility.reshape(NB, BLK),
    )
    return velocity, nearness.reshape(SEG)


def solution(mesh):
    in_specs = (
        P(None, "cells"),
        P(None, "cells"),
        P(None, "cells"),
        P("cells", "lanes"),
        P(None, "cells"),
        P(None, "cells"),
        P("cells"),
        P("cells"),
        P("cells"),
    )
    out_specs = (P(None, "cells"), P("cells"))
    return jax.shard_map(local, mesh=mesh, in_specs=in_specs, out_specs=out_specs, check_vma=False)
```

```python
import functools
import math

import jax
import jax.numpy as jnp
from jax import lax
from jax.experimental import pallas as pl
from jax.experimental.pallas import tpu as pltpu
from jax.sharding import PartitionSpec as P

BLK = 128
NB = 8
SEG = BLK * NB
HALF = NB // 2
NENT = 8
NCAND = 32
WIDE = 2
FAR = 3
SPAN = 2 * FAR + 1
FORCE_SCALE = 0.02
CORE_SQUARE = 0.25
TIME_STEP = 4.0
CENTRE = 2.0
TOGETHER = 16
SOONER = 4
AHEAD = 8
ABREAST = 4
F32 = jnp.float32
BF16 = jnp.bfloat16
MESH = pl.DeviceIdType.MESH
NN = (((1,), (0,)), ((), ()))


def rounded(x):
    return x.astype(BF16).astype(F32)


def two_parts(x):
    top = rounded(x)
    return top, rounded(x - top)


def three_parts(x):
    top = rounded(x)
    rest = x - top
    mid = rounded(rest)
    return top, mid, rounded(rest - mid)


def kernel(
    n_cells,
    lists_hbm,
    cand_t_hbm,
    cand_s_hbm,
    centres_hbm,
    lines_hbm,
    burgers_hbm,
    nodes_hbm,
    owner_hbm,
    mobility_hbm,
    velocity_out,
    nearness_out,
    win_c,
    win_l,
    win_b,
    nodes,
    owner,
    codes_r,
    cand_t,
    cand_s,
    mobility,
    list_own,
    list_far_v,
    list_far,
    dense,
    stage_f,
    stage_p,
    stage_q,
    stage_a,
    stage_n,
    stage_t,
    feat,
    pull,
    target,
    goal,
    codes_d,
    onehot,
    mask16,
    drag_send,
    drag_recv,
    eff,
    fbuf,
    vel,
    local_sem,
    send_a,
    recv_a,
    send_n,
    recv_n,
    misc_sem,
    send_b,
    recv_b,
):
    me = lax.axis_index("cells")
    lane = lax.axis_index("lanes")
    other = 1 - lane

    def cell(offset):
        return lax.rem(me + (offset + n_cells), n_cells)

    partners = [
        (o, far) for o in (3, -3, 2, -2, 1, -1, 0) for far in (True, False) if (o, far) != (0, False)
    ]

    greeted = [(o, False) for o in (3, -3, 2, -2, 1, -1)] + [(0, True)]
    barrier = pltpu.get_barrier_semaphore()
    for o, far in greeted:
        pl.semaphore_signal(
            barrier, inc=1, device_id=(cell(o), other if far else lane), device_id_type=MESH
        )
    own_copies = [
        pltpu.make_async_copy(centres_hbm, win_c, local_sem.at[0]),
        pltpu.make_async_copy(lines_hbm, win_l, local_sem.at[1]),
        pltpu.make_async_copy(burgers_hbm, win_b, local_sem.at[2]),
        pltpu.make_async_copy(nodes_hbm, nodes, local_sem.at[3]),
        pltpu.make_async_copy(owner_hbm, owner, local_sem.at[4]),
        pltpu.make_async_copy(lists_hbm, list_own, local_sem.at[5]),
        pltpu.make_async_copy(mobility_hbm, mobility, local_sem.at[6]),
        pltpu.make_async_copy(cand_t_hbm, cand_t, local_sem.at[7]),
        pltpu.make_async_copy(cand_s_hbm, cand_s, local_sem.at[8]),
    ]
    for copy in own_copies:
        copy.start()
    for copy in own_copies:
        copy.wait()

    for a, win in enumerate((win_c, win_l, win_b)):
        for b in range(NB):
            dense[WIDE, pl.ds(24 * a + b, 3, stride=NB), :] = win[:, b * BLK : (b + 1) * BLK]
    codes_r[FAR] = nodes[...] + SEG * owner[...]
    pl.semaphore_wait(barrier, len(greeted))

    def remote(src, dst, send, recv, o, far):
        return pltpu.make_async_remote_copy(
            src_ref=src,
            dst_ref=dst,
            send_sem=send,
            recv_sem=recv,
            device_id=(cell(o), other if far else lane),
            device_id_type=MESH,
        )

    list_copy = remote(lists_hbm, list_far_v, misc_sem.at[0], misc_sem.at[1], 0, True)
    list_copy.start()
    sends_a = {}
    for o in (-2, -1, 2, 1):
        slot = WIDE - o
        sends_a[o] = remote(
            dense.at[WIDE], dense.at[slot], send_a.at[WIDE + o], recv_a.at[slot], o, False
        )
        sends_a[o].start()
    sends_n = {}
    for o in (-3, -2, -1, 3, 2, 1):
        slot = FAR - o
        sends_n[o] = remote(
            codes_r.at[FAR], codes_r.at[slot], send_n.at[FAR + o], recv_n.at[slot], o, False
        )
        sends_n[o].start()

    def build_codes(slot):
        lanes = lax.broadcasted_iota(jnp.int32, (BLK, BLK), 1).astype(F32)
        for e in range(2):
            node = codes_r[slot, e : e + 1, :]
            high = lax.shift_right_logical(node, 7)
            rows16 = lax.broadcasted_iota(jnp.int32, (16, SEG), 0)
            mask16[slot, :, pl.ds(e * SEG, SEG)] = (rows16 == high).astype(F32)
            for b in range(NB):
                codes_d[slot, e, b : b + 1, :] = node[:, b * BLK : (b + 1) * BLK]
            low = jnp.bitwise_and(codes_d[slot, e], BLK - 1).astype(F32)
            turned = jnp.transpose(low)
            for b in range(NB):
                column = jnp.broadcast_to(turned[:, b : b + 1], (BLK, BLK))
                rows = pl.ds(e * SEG + b * BLK, BLK)
                onehot[slot, rows, :] = (column == lanes).astype(F32).astype(BF16)

    ones = jnp.ones((NB, BLK), F32)
    zeros = jnp.zeros((NB, BLK), F32)

    def odd(rows):
        return len(rows) | 1

    def put(ref, base, rows):
        for r, row in enumerate(rows):
            ref[pl.ds(base * odd(rows) + r, NB, stride=odd(rows)), :] = row

    def dense_fields(s):
        parts = [dense[s, NB * k : NB * (k + 1), :] for k in range(9)]
        return [x - CENTRE for x in parts[0:3]], parts[3:6], parts[6:9]

    def dot3(x, y):
        return x[0] * y[0] + x[1] * y[1] + x[2] * y[2]

    def split3(rows):
        return [list(x) for x in zip(*(three_parts(row) for row in rows))]

    def split2(rows):
        return [list(x) for x in zip(*(two_parts(row) for row in rows))]

    def build_source(s):
        c, line, burg = dense_fields(s)
        ch, cm, cl = split3(c)
        sh, sm, sl = three_parts(dot3(c, c) + CORE_SQUARE)
        bh, bm = split2(burg)
        rows = ch + cm + [sh, sm] + ch + cm + [ones, ones] + cl + ch + [sl, ones]
        rows += (bh + bm + [zeros, zeros]) * 2 + [zeros] * 8
        put(stage_f, s * NB, rows)
        moment = [
            line[1] * c[2] - line[2] * c[1],
            line[2] * c[0] - line[0] * c[2],
            line[0] * c[1] - line[1] * c[0],
        ]
        high, low = split2(line + moment)
        put(stage_p, s * NB, high + [zeros, zeros] + low + [zeros, zeros])
        for b in range(s * NB, (s + 1) * NB):
            feat[b] = jnp.transpose(stage_f[49 * b : 49 * b + 48, :]).astype(BF16)
            pulls = stage_p[17 * b : 17 * b + 16, :].astype(BF16)
            pull[b] = jnp.concatenate([pulls, pulls], axis=1)
        return c, line, (ch, cm, cl), (sh, sm)

    centre_own, line_own, (ch, cm, cl), own_square = build_source(WIDE)

    def twice(rows):
        return [-2.0 * row for row in rows]

    zh, zm, zl = three_parts(dot3(centre_own, centre_own))
    lh, lm = split2(line_own)
    rows = twice(ch) * 2 + [ones, ones] + twice(cm) * 2 + [zh, zm]
    rows += twice(ch) + twice(cl) + [ones, zl]
    put(stage_q, 0, rows)
    put(stage_a, 0, lh * 2 + [zeros, zeros] + lm * 2 + [zeros, zeros])
    for b in range(NB):
        right = jnp.concatenate([stage_q[25 * b : 25 * b + 24, :], jnp.zeros((24, BLK), F32)], 0)
        target[b, :, 0:BLK] = right.astype(BF16)
        right = jnp.concatenate(
            [
                jnp.zeros((24, BLK), F32),
                stage_a[17 * b : 17 * b + 16, :],
                jnp.zeros((8, BLK), F32),
            ],
            0,
        )
        target[b, :, BLK : 2 * BLK] = right.astype(BF16)

    build_codes(FAR)
    line = [win_l[k : k + 1, :] for k in range(3)]
    length = 0.5 * jnp.sqrt(dot3(line, line))
    drag = jnp.zeros((32, BLK), F32)
    for e in range(2):
        span = slice(e * SEG, (e + 1) * SEG)
        mask = mask16[FAR, :, span] > 0.5
        parts = [
            jnp.where(mask, jnp.broadcast_to(part, (16, SEG)), 0.0) for part in two_parts(length)
        ]
        drag = drag + lax.dot_general(
            jnp.concatenate(parts, axis=0).astype(BF16),
            onehot[FAR, span, :],
            NN,
            preferred_element_type=F32,
        )
    drag_send[...] = drag[8:16] + drag[24:32]
    drag_copy = remote(drag_send, drag_recv, misc_sem.at[2], misc_sem.at[3], 1, False)
    drag_copy.start()
    own_drag = drag[0:8] + drag[16:24]

    kept_centres = {0: (centre_own, line_own, (ch, cm, cl), own_square)}

    def sources_of(pair):
        for o in pair:
            sends_a[-o].wait_recv()
        for o in pair:
            kept_centres[o] = build_source(WIDE + o)

    sources_of((-1, -2))
    list_copy.wait_recv()
    to_smem = pltpu.make_async_copy(list_far_v, list_far, misc_sem.at[4])
    to_smem.start()
    to_smem.wait()
    drag_copy.wait_recv()
    eff_all = mobility[...] / (1.0 + (own_drag + drag_recv[...]))
    for b in range(NB):
        eff[b] = eff_all[b : b + 1, :]
    sources_of((1, 2))

    def some_targets(t, carry):
        blocks = [HALF * lane + t * ABREAST + k for k in range(ABREAST)]
        rights = [target[block] for block in blocks]
        totals = [jnp.zeros((16, BLK), F32) for block in blocks]
        sources = [
            (k, lists[block, e])
            for k, block in enumerate(blocks)
            for lists in (list_own, list_far)
            for e in range(NENT)
        ]
        ahead = []
        for n in range(len(sources) + AHEAD):
            if n < len(sources):
                k, source = sources[n]
                ahead.append(
                    lax.dot_general(feat[source], rights[k], NN, preferred_element_type=F32)
                )
            if n < AHEAD:
                continue
            both = ahead[n - AHEAD]
            inverse = lax.rsqrt(both[:, 0:BLK])
            weight = both[:, BLK : 2 * BLK] * inverse * inverse * inverse
            top = weight.astype(BF16)
            low = (weight - top.astype(F32)).astype(BF16)
            k, source = sources[n - AHEAD]
            totals[k] = totals[k] + lax.dot_general(
                pull[source],
                jnp.concatenate([top, low], axis=0),
                NN,
                preferred_element_type=F32,
            )
        for block, total in zip(blocks, totals):
            total = total[0:8] + total[8:16]
            cut = pl.ds(pl.multiple_of(block * BLK, BLK), BLK)
            x, y, z = (win_c[k : k + 1, cut] - CENTRE for k in range(3))
            sx, sy, sz = (total[k : k + 1] for k in range(3))
            scale = 0.5 * FORCE_SCALE
            fbuf[FAR, block, 0:1, :] = scale * (sy * z - sz * y - total[3:4])
            fbuf[FAR, block, 1:2, :] = scale * (sz * x - sx * z - total[4:5])
            fbuf[FAR, block, 2:3, :] = scale * (sx * y - sy * x - total[5:6])
            fbuf[FAR, block, 3:4, :] = eff[block]
        return carry

    lax.fori_loop(0, HALF // ABREAST, some_targets, 0)

    for copy in sends_n.values():
        copy.wait_recv()

    mine = pl.ds(HALF * lane, HALF)
    sends_b = []
    for o, far in partners:
        slot = FAR - o
        copy = remote(
            fbuf.at[FAR, mine],
            fbuf.at[slot, mine],
            send_b.at[FAR + o, int(far)],
            recv_b.at[slot, int(far)],
            o,
            far,
        )
        copy.start()
        sends_b.append(copy)

    for o in (1, -1, 2, -2, 3, -3):
        build_codes(FAR + o)
    for copy in list(sends_a.values()) + list(sends_n.values()) + [list_copy, drag_copy]:
        copy.wait_send()

    own_part = {}
    next_part = {}
    recv_of = dict(zip(partners, sends_b))

    def wait_forces(o):
        for far in (False, True):
            if (-o, far) in recv_of:
                recv_of[(-o, far)].wait_recv()

    def scatter(o):
        slot = FAR + o
        forces = jnp.concatenate([fbuf[slot, b] for b in range(NB)], axis=1)
        parts = two_parts(forces)
        first = NB if o == -FAR else 0
        last = NB if o == FAR else 2 * NB
        size = last - first
        total = jnp.zeros((6 * size, BLK), F32)
        for e in range(2):
            span = slice(e * SEG, (e + 1) * SEG)
            mask = mask16[slot, first:last, span] > 0.5
            stack = [
                jnp.where(mask, jnp.broadcast_to(part[k : k + 1], (size, SEG)), 0.0)
                for part in parts
                for k in range(3)
            ]
            total = total + lax.dot_general(
                jnp.concatenate(stack, axis=0).astype(BF16),
                onehot[slot, span, :],
                NN,
                preferred_element_type=F32,
            )
        total = total[0 : 3 * size] + total[3 * size : 6 * size]
        if o < FAR:
            next_part[o] = [total[size * (k + 1) - NB : size * (k + 1)] for k in range(3)]
        if o > -FAR:
            own_part[o] = [total[size * k : size * k + NB] for k in range(3)]

    def node_velocity(o):
        eff_o = jnp.concatenate([fbuf[FAR + o, b, 3:4, :] for b in range(NB)], axis=0)
        for k in range(3):
            value = eff_o * (own_part[o][k] + next_part[o - 1][k])
            vel[FAR + o, k] = value
            if o == 0:
                for b in range(NB):
                    velocity_out[k : k + 1, b * BLK : (b + 1) * BLK] = value[b : b + 1, :]

    shift = []
    early = {}

    def gather(o):
        slot = FAR + o
        s = WIDE + o
        moved = [zeros, zeros, zeros]
        for e in range(2):
            code = codes_d[slot, e]
            low = jnp.bitwise_and(code, BLK - 1)
            high = lax.shift_right_logical(code, 7)
            picked = early.get((o, e), [zeros, zeros, zeros])
            for h in range(NB if (o, e) in early else 2 * NB):
                here = high == h
                for k in range(3):
                    row = vel[slot + h // NB, k, h % NB : h % NB + 1, :]
                    table = jnp.broadcast_to(row, (NB, BLK))
                    found = jnp.take_along_axis(table, low, axis=1, mode="promise_in_bounds")
                    picked[k] = jnp.where(here, found, picked[k])
            moved = [x + y for x, y in zip(moved, picked)]
        moved = [0.5 * TIME_STEP * x for x in moved]
        if not shift:
            shift.extend(
                jnp.sum(jnp.sum(x, axis=1, keepdims=True), axis=0, keepdims=True) / SEG
                for x in moved
            )
        moved = [x - jnp.broadcast_to(y, (NB, BLK)) for x, y in zip(moved, shift)]
        c, unused, (ch, cm, cl), (sh, sm) = kept_centres[o]
        vh, vl = split2(moved)
        ph, pm = two_parts(dot3(c, moved))
        speed = dot3(moved, moved)
        mh, ml = two_parts(speed + CORE_SQUARE)
        rows = vh + vl + [ph, pm] + vh + vl + [ones, ones]
        rows += ch + cm + [mh, ml] + ch + cm + [sh, sm]
        put(stage_n, s * NB, rows)
        if o == 0:
            kh, kl = two_parts(speed)
            zh, zm = two_parts(dot3(c, c))
            none = [zeros, zeros]
            rows = ch * 2 + [-ones, -ones] + cm * 2 + [-ph, -pm] + vh * 2 + none + vl * 2 + none
            put(stage_t, 0, rows)
            rows = twice(vh) * 2 + none + twice(vl) * 2 + [kh, kl]
            rows += [zeros] * 6 + [ones, ones] + [zeros] * 8
            put(stage_t, NB, rows)
            rows = [zeros] * 14 + [zh, zm] + twice(ch) * 2 + none + twice(cm) * 2 + [ones, ones]
            put(stage_t, 2 * NB, rows)
            for b in range(NB):
                for g in range(3):
                    rows_of = pl.ds(33 * (g * NB + b), 32)
                    goal[b, :, g * BLK : (g + 1) * BLK] = stage_t[rows_of, :].astype(BF16)

    def gather_early():
        for e in range(2):
            code = codes_d[FAR, e]
            low = jnp.bitwise_and(code, BLK - 1)
            high = lax.shift_right_logical(code, 7)
            picked = [zeros, zeros, zeros]
            for h in range(NB):
                here = high == NB + h
                for k in range(3):
                    table = jnp.broadcast_to(vel[FAR + 1, k, h : h + 1, :], (NB, BLK))
                    found = jnp.take_along_axis(table, low, axis=1, mode="promise_in_bounds")
                    picked[k] = jnp.where(here, found, picked[k])
            early[(0, e)] = picked

    for o in (0, 1, 2, 3):
        wait_forces(o)
    for o in (0, 1, 2, 3):
        scatter(o)
    for o in (1, 2, 3):
        node_velocity(o)
    for o in (1, 2):
        gather(o)
    gather_early()
    for o in (-1, -2, -3):
        wait_forces(o)
    for o in (-1, -2, -3):
        scatter(o)
    for o in (0, -1, -2):
        node_velocity(o)
    for o in (0, -1, -2):
        gather(o)

    block_rows = lax.broadcasted_iota(jnp.int32, (NB, BLK), 0)

    def some_pairs(n, near):
        pairs = [(cand_t[TOGETHER * n + k], cand_s[TOGETHER * n + k]) for k in range(TOGETHER)]
        dots = []
        for k in range(TOGETHER + SOONER):
            if k < TOGETHER:
                into, source = pairs[k]
                there = jnp.transpose(stage_n[pl.ds(source * 33, 32), :]).astype(BF16)
                dots.append(lax.dot_general(there, goal[into], NN, preferred_element_type=F32))
            if k < SOONER:
                continue
            into, both = pairs[k - SOONER][0], dots[k - SOONER]
            ahead = both[:, 0:BLK]
            square = both[:, BLK : 2 * BLK]
            kept = jnp.minimum(jnp.maximum(ahead, 0.0), square)
            fraction = kept / square
            near_by = jnp.exp(
                fraction * (2.0 * ahead - kept + CORE_SQUARE * fraction) - both[:, 2 * BLK :]
            )
            row = jnp.sum(near_by, axis=0, keepdims=True)
            near = near + jnp.where(block_rows == into, jnp.broadcast_to(row, (NB, BLK)), 0.0)
        return near

    near = lax.fori_loop(0, NCAND // TOGETHER, some_pairs, jnp.zeros((NB, BLK), F32))
    nearness_out[...] = math.exp(CORE_SQUARE) * near

    for copy in sends_b:
        copy.wait_send()


def local(
    centres,
    seg_lines,
    burgers,
    neighbour_blocks,
    seg_nodes,
    node_owner,
    mobility,
    cand_target,
    cand_source,
):
    n_cells = lax.axis_size("cells")
    window = 2 * WIDE + 1
    hbm = pl.BlockSpec(memory_space=pltpu.HBM)
    vmem = pl.BlockSpec(memory_space=pltpu.VMEM)
    velocity, nearness = pl.pallas_call(
        functools.partial(kernel, n_cells),
        name="dislocation_step",
        out_shape=(
            pltpu.VMEM((3, SEG), F32),
            pltpu.VMEM((NB, BLK), F32),
        ),
        in_specs=[hbm] * 9,
        out_specs=(vmem, vmem),
        scratch_shapes=[
            pltpu.VMEM((3, SEG), F32),
            pltpu.VMEM((3, SEG), F32),
            pltpu.VMEM((3, SEG), F32),
            pltpu.VMEM((2, SEG), jnp.int32),
            pltpu.VMEM((2, SEG), jnp.int32),
            pltpu.VMEM((SPAN, 2, SEG), jnp.int32),
            pltpu.SMEM((NCAND,), jnp.int32),
            pltpu.SMEM((NCAND,), jnp.int32),
            pltpu.VMEM((NB, BLK), F32),
            pltpu.SMEM((NB, NENT), jnp.int32),
            pltpu.VMEM((NB, NENT), jnp.int32),
            pltpu.SMEM((NB, NENT), jnp.int32),
            pltpu.VMEM((window, 72, BLK), F32),
            pltpu.VMEM((window * NB * 49, BLK), F32),
            pltpu.VMEM((window * NB * 17, BLK), F32),
            pltpu.VMEM((NB * 25, BLK), F32),
            pltpu.VMEM((NB * 17, BLK), F32),
            pltpu.VMEM((window * NB * 33, BLK), F32),
            pltpu.VMEM((3 * NB * 33, BLK), F32),
            pltpu.VMEM((window * NB, BLK, 48), BF16),
            pltpu.VMEM((window * NB, 16, 2 * BLK), BF16),
            pltpu.VMEM((NB, 48, 2 * BLK), BF16),
            pltpu.VMEM((NB, 32, 3 * BLK), BF16),
            pltpu.VMEM((SPAN, 2, NB, BLK), jnp.int32),
            pltpu.VMEM((SPAN, 2 * SEG, BLK), BF16),
            pltpu.VMEM((SPAN, 16, 2 * SEG), F32),
            pltpu.VMEM((NB, BLK), F32),
            pltpu.VMEM((NB, BLK), F32),
            pltpu.VMEM((NB, 1, BLK), F32),
            pltpu.VMEM((SPAN, NB, 4, BLK), F32),
            pltpu.VMEM((SPAN, 3, NB, BLK), F32),
            pltpu.SemaphoreType.DMA((9,)),
            pltpu.SemaphoreType.DMA((window,)),
            pltpu.SemaphoreType.DMA((window,)),
            pltpu.SemaphoreType.DMA((SPAN,)),
            pltpu.SemaphoreType.DMA((SPAN,)),
            pltpu.SemaphoreType.DMA((5,)),
            pltpu.SemaphoreType.DMA((SPAN, 2)),
            pltpu.SemaphoreType.DMA((SPAN, 2)),
        ],
        compiler_params=pltpu.CompilerParams(
            collective_id=0, has_side_effects=True, vmem_limit_bytes=60 * 1024 * 1024
        ),
    )(
        neighbour_blocks,
        cand_target,
        cand_source,
        centres,
        seg_lines,
        burgers,
        seg_nodes,
        node_owner,
        mobility.reshape(NB, BLK),
    )
    return velocity, nearness.reshape(SEG)


def solution(mesh):
    in_specs = (
        P(None, "cells"),
        P(None, "cells"),
        P(None, "cells"),
        P("cells", "lanes"),
        P(None, "cells"),
        P(None, "cells"),
        P("cells"),
        P("cells"),
        P("cells"),
    )
    out_specs = (P(None, "cells"), P("cells"))
    return jax.shard_map(local, mesh=mesh, in_specs=in_specs, out_specs=out_specs, check_vma=False)
```

```python
import functools
import math

import jax
import jax.numpy as jnp
from jax import lax
from jax.experimental import pallas as pl
from jax.experimental.pallas import tpu as pltpu
from jax.sharding import PartitionSpec as P

BLK = 128
NB = 8
SEG = BLK * NB
HALF = NB // 2
NENT = 8
NCAND = 32
WIDE = 2
FAR = 3
SPAN = 2 * FAR + 1
FORCE_SCALE = 0.02
CORE_SQUARE = 0.25
TIME_STEP = 4.0
CENTRE = 2.0
TOGETHER = 16
SOONER = 4
AHEAD = 8
ABREAST = 4
F32 = jnp.float32
BF16 = jnp.bfloat16
MESH = pl.DeviceIdType.MESH
NN = (((1,), (0,)), ((), ()))


def rounded(x):
    return x.astype(BF16).astype(F32)


def two_parts(x):
    top = rounded(x)
    return top, rounded(x - top)


def three_parts(x):
    top = rounded(x)
    rest = x - top
    mid = rounded(rest)
    return top, mid, rounded(rest - mid)


def kernel(
    n_cells,
    lists_hbm,
    cand_t_hbm,
    cand_s_hbm,
    centres_hbm,
    lines_hbm,
    burgers_hbm,
    nodes_hbm,
    owner_hbm,
    mobility_hbm,
    velocity_out,
    nearness_out,
    win_c,
    win_l,
    win_b,
    nodes,
    owner,
    codes_r,
    cand_t,
    cand_s,
    mobility,
    list_own,
    list_far_v,
    list_far,
    dense,
    stage_f,
    stage_p,
    stage_q,
    stage_a,
    stage_n,
    stage_t,
    feat,
    pull,
    target,
    goal,
    codes_d,
    onehot,
    mask16,
    drag_send,
    drag_recv,
    eff,
    fbuf,
    vel,
    local_sem,
    send_a,
    recv_a,
    send_n,
    recv_n,
    misc_sem,
    send_b,
    recv_b,
):
    me = lax.axis_index("cells")
    lane = lax.axis_index("lanes")
    other = 1 - lane

    def cell(offset):
        return lax.rem(me + (offset + n_cells), n_cells)

    partners = [
        (o, far) for o in (3, -3, 2, -2, 1, -1, 0) for far in (True, False) if (o, far) != (0, False)
    ]

    greeted = [(o, False) for o in (3, -3, 2, -2, 1, -1)] + [(0, True)]
    barrier = pltpu.get_barrier_semaphore()
    for o, far in greeted:
        pl.semaphore_signal(
            barrier, inc=1, device_id=(cell(o), other if far else lane), device_id_type=MESH
        )
    own_copies = [
        pltpu.make_async_copy(centres_hbm, win_c, local_sem.at[0]),
        pltpu.make_async_copy(lines_hbm, win_l, local_sem.at[1]),
        pltpu.make_async_copy(burgers_hbm, win_b, local_sem.at[2]),
        pltpu.make_async_copy(nodes_hbm, nodes, local_sem.at[3]),
        pltpu.make_async_copy(owner_hbm, owner, local_sem.at[4]),
        pltpu.make_async_copy(lists_hbm, list_own, local_sem.at[5]),
        pltpu.make_async_copy(mobility_hbm, mobility, local_sem.at[6]),
        pltpu.make_async_copy(cand_t_hbm, cand_t, local_sem.at[7]),
        pltpu.make_async_copy(cand_s_hbm, cand_s, local_sem.at[8]),
    ]
    for copy in own_copies:
        copy.start()
    for copy in own_copies:
        copy.wait()

    for a, win in enumerate((win_c, win_l, win_b)):
        for b in range(NB):
            dense[WIDE, pl.ds(24 * a + b, 3, stride=NB), :] = win[:, b * BLK : (b + 1) * BLK]
    codes_r[FAR] = nodes[...] + SEG * owner[...]
    pl.semaphore_wait(barrier, len(greeted))

    def remote(src, dst, send, recv, o, far):
        return pltpu.make_async_remote_copy(
            src_ref=src,
            dst_ref=dst,
            send_sem=send,
            recv_sem=recv,
            device_id=(cell(o), other if far else lane),
            device_id_type=MESH,
        )

    list_copy = remote(lists_hbm, list_far_v, misc_sem.at[0], misc_sem.at[1], 0, True)
    list_copy.start()
    sends_a = {}
    for o in (-2, -1, 2, 1):
        slot = WIDE - o
        sends_a[o] = remote(
            dense.at[WIDE], dense.at[slot], send_a.at[WIDE + o], recv_a.at[slot], o, False
        )
        sends_a[o].start()
    sends_n = {}
    for o in (-3, -2, -1, 3, 2, 1):
        slot = FAR - o
        sends_n[o] = remote(
            codes_r.at[FAR], codes_r.at[slot], send_n.at[FAR + o], recv_n.at[slot], o, False
        )
        sends_n[o].start()

    def build_codes(slot):
        lanes = lax.broadcasted_iota(jnp.int32, (BLK, BLK), 1).astype(F32)
        for e in range(2):
            node = codes_r[slot, e : e + 1, :]
            high = lax.shift_right_logical(node, 7)
            rows16 = lax.broadcasted_iota(jnp.int32, (16, SEG), 0)
            mask16[slot, :, pl.ds(e * SEG, SEG)] = (rows16 == high).astype(F32)
            for b in range(NB):
                codes_d[slot, e, b : b + 1, :] = node[:, b * BLK : (b + 1) * BLK]
            low = jnp.bitwise_and(codes_d[slot, e], BLK - 1).astype(F32)
            turned = jnp.transpose(low)
            for b in range(NB):
                column = jnp.broadcast_to(turned[:, b : b + 1], (BLK, BLK))
                rows = pl.ds(e * SEG + b * BLK, BLK)
                onehot[slot, rows, :] = (column == lanes).astype(F32).astype(BF16)

    ones = jnp.ones((NB, BLK), F32)
    zeros = jnp.zeros((NB, BLK), F32)

    def odd(rows):
        return len(rows) | 1

    def put(ref, base, rows):
        for r, row in enumerate(rows):
            ref[pl.ds(base * odd(rows) + r, NB, stride=odd(rows)), :] = row

    def dense_fields(s):
        parts = [dense[s, NB * k : NB * (k + 1), :] for k in range(9)]
        return [x - CENTRE for x in parts[0:3]], parts[3:6], parts[6:9]

    def dot3(x, y):
        return x[0] * y[0] + x[1] * y[1] + x[2] * y[2]

    def split3(rows):
        return [list(x) for x in zip(*(three_parts(row) for row in rows))]

    def split2(rows):
        return [list(x) for x in zip(*(two_parts(row) for row in rows))]

    def build_source(s):
        c, line, burg = dense_fields(s)
        ch, cm, cl = split3(c)
        sh, sm, sl = three_parts(dot3(c, c) + CORE_SQUARE)
        bh, bm = split2(burg)
        rows = ch + cm + [sh, sm] + ch + cm + [ones, ones] + cl + ch + [sl, ones]
        rows += (bh + bm + [zeros, zeros]) * 2 + [zeros] * 8
        put(stage_f, s * NB, rows)
        moment = [
            line[1] * c[2] - line[2] * c[1],
            line[2] * c[0] - line[0] * c[2],
            line[0] * c[1] - line[1] * c[0],
        ]
        high, low = split2(line + moment)
        put(stage_p, s * NB, high + [zeros, zeros] + low + [zeros, zeros])
        for b in range(s * NB, (s + 1) * NB):
            feat[b] = jnp.transpose(stage_f[49 * b : 49 * b + 48, :]).astype(BF16)
            pulls = stage_p[17 * b : 17 * b + 16, :].astype(BF16)
            pull[b] = jnp.concatenate([pulls, pulls], axis=1)
        return c, line, (ch, cm, cl), (sh, sm)

    centre_own, line_own, (ch, cm, cl), own_square = build_source(WIDE)

    def twice(rows):
        return [-2.0 * row for row in rows]

    zh, zm, zl = three_parts(dot3(centre_own, centre_own))
    lh, lm = split2(line_own)
    rows = twice(ch) * 2 + [ones, ones] + twice(cm) * 2 + [zh, zm]
    rows += twice(ch) + twice(cl) + [ones, zl]
    put(stage_q, 0, rows)
    put(stage_a, 0, lh * 2 + [zeros, zeros] + lm * 2 + [zeros, zeros])
    for b in range(NB):
        right = jnp.concatenate([stage_q[25 * b : 25 * b + 24, :], jnp.zeros((24, BLK), F32)], 0)
        target[b, :, 0:BLK] = right.astype(BF16)
        right = jnp.concatenate(
            [
                jnp.zeros((24, BLK), F32),
                stage_a[17 * b : 17 * b + 16, :],
                jnp.zeros((8, BLK), F32),
            ],
            0,
        )
        target[b, :, BLK : 2 * BLK] = right.astype(BF16)

    build_codes(FAR)
    line = [win_l[k : k + 1, :] for k in range(3)]
    length = 0.5 * jnp.sqrt(dot3(line, line))
    drag = jnp.zeros((32, BLK), F32)
    for e in range(2):
        span = slice(e * SEG, (e + 1) * SEG)
        mask = mask16[FAR, :, span] > 0.5
        parts = [
            jnp.where(mask, jnp.broadcast_to(part, (16, SEG)), 0.0) for part in two_parts(length)
        ]
        drag = drag + lax.dot_general(
            jnp.concatenate(parts, axis=0).astype(BF16),
            onehot[FAR, span, :],
            NN,
            preferred_element_type=F32,
        )
    drag_send[...] = drag[8:16] + drag[24:32]
    drag_copy = remote(drag_send, drag_recv, misc_sem.at[2], misc_sem.at[3], 1, False)
    drag_copy.start()
    own_drag = drag[0:8] + drag[16:24]

    kept_centres = {0: (centre_own, line_own, (ch, cm, cl), own_square)}

    def sources_of(pair):
        for o in pair:
            sends_a[-o].wait_recv()
        for o in pair:
            kept_centres[o] = build_source(WIDE + o)

    sources_of((-1, -2))
    list_copy.wait_recv()
    to_smem = pltpu.make_async_copy(list_far_v, list_far, misc_sem.at[4])
    to_smem.start()
    to_smem.wait()
    drag_copy.wait_recv()
    eff_all = mobility[...] / (1.0 + (own_drag + drag_recv[...]))
    for b in range(NB):
        eff[b] = eff_all[b : b + 1, :]
    sources_of((2,))
    sources_of((1,))

    def some_targets(t, carry):
        blocks = [HALF * lane + t * ABREAST + k for k in range(ABREAST)]
        rights = [target[block] for block in blocks]
        totals = [jnp.zeros((16, BLK), F32) for block in blocks]
        sources = [
            (k, lists[block, e])
            for k, block in enumerate(blocks)
            for lists in (list_own, list_far)
            for e in range(NENT)
        ]
        ahead = []
        for n in range(len(sources) + AHEAD):
            if n < len(sources):
                k, source = sources[n]
                ahead.append(
                    lax.dot_general(feat[source], rights[k], NN, preferred_element_type=F32)
                )
            if n < AHEAD:
                continue
            both = ahead[n - AHEAD]
            inverse = lax.rsqrt(both[:, 0:BLK])
            weight = both[:, BLK : 2 * BLK] * inverse * inverse * inverse
            top = weight.astype(BF16)
            low = (weight - top.astype(F32)).astype(BF16)
            k, source = sources[n - AHEAD]
            totals[k] = totals[k] + lax.dot_general(
                pull[source],
                jnp.concatenate([top, low], axis=0),
                NN,
                preferred_element_type=F32,
            )
        for block, total in zip(blocks, totals):
            total = total[0:8] + total[8:16]
            cut = pl.ds(pl.multiple_of(block * BLK, BLK), BLK)
            x, y, z = (win_c[k : k + 1, cut] - CENTRE for k in range(3))
            sx, sy, sz = (total[k : k + 1] for k in range(3))
            scale = 0.5 * FORCE_SCALE
            fbuf[FAR, block, 0:1, :] = scale * (sy * z - sz * y - total[3:4])
            fbuf[FAR, block, 1:2, :] = scale * (sz * x - sx * z - total[4:5])
            fbuf[FAR, block, 2:3, :] = scale * (sx * y - sy * x - total[5:6])
            fbuf[FAR, block, 3:4, :] = eff[block]
        return carry

    lax.fori_loop(0, HALF // ABREAST, some_targets, 0)

    for copy in sends_n.values():
        copy.wait_recv()

    mine = pl.ds(HALF * lane, HALF)
    sends_b = []
    for o, far in partners:
        slot = FAR - o
        copy = remote(
            fbuf.at[FAR, mine],
            fbuf.at[slot, mine],
            send_b.at[FAR + o, int(far)],
            recv_b.at[slot, int(far)],
            o,
            far,
        )
        copy.start()
        sends_b.append(copy)

    for o in (1, -1, 2, -2, 3, -3):
        build_codes(FAR + o)
    for copy in list(sends_a.values()) + list(sends_n.values()) + [list_copy, drag_copy]:
        copy.wait_send()

    own_part = {}
    next_part = {}
    recv_of = dict(zip(partners, sends_b))

    def wait_forces(o):
        for far in (False, True):
            if (-o, far) in recv_of:
                recv_of[(-o, far)].wait_recv()

    def scatter(o):
        slot = FAR + o
        forces = jnp.concatenate([fbuf[slot, b] for b in range(NB)], axis=1)
        parts = two_parts(forces)
        first = NB if o == -FAR else 0
        last = NB if o == FAR else 2 * NB
        size = last - first
        total = jnp.zeros((6 * size, BLK), F32)
        for e in range(2):
            span = slice(e * SEG, (e + 1) * SEG)
            mask = mask16[slot, first:last, span] > 0.5
            stack = [
                jnp.where(mask, jnp.broadcast_to(part[k : k + 1], (size, SEG)), 0.0)
                for part in parts
                for k in range(3)
            ]
            total = total + lax.dot_general(
                jnp.concatenate(stack, axis=0).astype(BF16),
                onehot[slot, span, :],
                NN,
                preferred_element_type=F32,
            )
        total = total[0 : 3 * size] + total[3 * size : 6 * size]
        if o < FAR:
            next_part[o] = [total[size * (k + 1) - NB : size * (k + 1)] for k in range(3)]
        if o > -FAR:
            own_part[o] = [total[size * k : size * k + NB] for k in range(3)]

    def node_velocity(o):
        eff_o = jnp.concatenate([fbuf[FAR + o, b, 3:4, :] for b in range(NB)], axis=0)
        for k in range(3):
            value = eff_o * (own_part[o][k] + next_part[o - 1][k])
            vel[FAR + o, k] = value
            if o == 0:
                for b in range(NB):
                    velocity_out[k : k + 1, b * BLK : (b + 1) * BLK] = value[b : b + 1, :]

    shift = []

    def gather(o):
        slot = FAR + o
        s = WIDE + o
        moved = [zeros, zeros, zeros]
        for e in range(2):
            code = codes_d[slot, e]
            low = jnp.bitwise_and(code, BLK - 1)
            high = lax.shift_right_logical(code, 7)
            picked = [zeros, zeros, zeros]
            for h in range(16):
                here = high == h
                for k in range(3):
                    row = vel[slot + h // NB, k, h % NB : h % NB + 1, :]
                    table = jnp.broadcast_to(row, (NB, BLK))
                    found = jnp.take_along_axis(table, low, axis=1, mode="promise_in_bounds")
                    picked[k] = jnp.where(here, found, picked[k])
            moved = [x + y for x, y in zip(moved, picked)]
        moved = [0.5 * TIME_STEP * x for x in moved]
        if not shift:
            shift.extend(
                jnp.sum(jnp.sum(x, axis=1, keepdims=True), axis=0, keepdims=True) / SEG
                for x in moved
            )
        moved = [x - jnp.broadcast_to(y, (NB, BLK)) for x, y in zip(moved, shift)]
        c, unused, (ch, cm, cl), (sh, sm) = kept_centres[o]
        vh, vl = split2(moved)
        ph, pm = two_parts(dot3(c, moved))
        speed = dot3(moved, moved)
        mh, ml = two_parts(speed + CORE_SQUARE)
        rows = vh + vl + [ph, pm] + vh + vl + [ones, ones]
        rows += ch + cm + [mh, ml] + ch + cm + [sh, sm]
        put(stage_n, s * NB, rows)
        if o == 0:
            kh, kl = two_parts(speed)
            zh, zm = two_parts(dot3(c, c))
            none = [zeros, zeros]
            rows = ch * 2 + [-ones, -ones] + cm * 2 + [-ph, -pm] + vh * 2 + none + vl * 2 + none
            put(stage_t, 0, rows)
            rows = twice(vh) * 2 + none + twice(vl) * 2 + [kh, kl]
            rows += [zeros] * 6 + [ones, ones] + [zeros] * 8
            put(stage_t, NB, rows)
            rows = [zeros] * 14 + [zh, zm] + twice(ch) * 2 + none + twice(cm) * 2 + [ones, ones]
            put(stage_t, 2 * NB, rows)
            for b in range(NB):
                for g in range(3):
                    rows_of = pl.ds(33 * (g * NB + b), 32)
                    goal[b, :, g * BLK : (g + 1) * BLK] = stage_t[rows_of, :].astype(BF16)

    for o in (0, 1, 2, 3):
        wait_forces(o)
    for o in (0, 1, 2, 3):
        scatter(o)
    for o in (1, 2, 3):
        node_velocity(o)
    for o in (1, 2):
        gather(o)
    for o in (-1, -2, -3):
        wait_forces(o)
    for o in (-1, -2, -3):
        scatter(o)
    for o in (0, -1, -2):
        node_velocity(o)
    for o in (0, -1, -2):
        gather(o)

    block_rows = lax.broadcasted_iota(jnp.int32, (NB, BLK), 0)

    def some_pairs(n, near):
        pairs = [(cand_t[TOGETHER * n + k], cand_s[TOGETHER * n + k]) for k in range(TOGETHER)]
        dots = []
        for k in range(TOGETHER + SOONER):
            if k < TOGETHER:
                into, source = pairs[k]
                there = jnp.transpose(stage_n[pl.ds(source * 33, 32), :]).astype(BF16)
                dots.append(lax.dot_general(there, goal[into], NN, preferred_element_type=F32))
            if k < SOONER:
                continue
            into, both = pairs[k - SOONER][0], dots[k - SOONER]
            ahead = both[:, 0:BLK]
            square = both[:, BLK : 2 * BLK]
            kept = jnp.minimum(jnp.maximum(ahead, 0.0), square)
            fraction = kept / square
            near_by = jnp.exp(
                fraction * (2.0 * ahead - kept + CORE_SQUARE * fraction) - both[:, 2 * BLK :]
            )
            row = jnp.sum(near_by, axis=0, keepdims=True)
            near = near + jnp.where(block_rows == into, jnp.broadcast_to(row, (NB, BLK)), 0.0)
        return near

    near = lax.fori_loop(0, NCAND // TOGETHER, some_pairs, jnp.zeros((NB, BLK), F32))
    nearness_out[...] = math.exp(CORE_SQUARE) * near

    for copy in sends_b:
        copy.wait_send()


def local(
    centres,
    seg_lines,
    burgers,
    neighbour_blocks,
    seg_nodes,
    node_owner,
    mobility,
    cand_target,
    cand_source,
):
    n_cells = lax.axis_size("cells")
    window = 2 * WIDE + 1
    hbm = pl.BlockSpec(memory_space=pltpu.HBM)
    vmem = pl.BlockSpec(memory_space=pltpu.VMEM)
    velocity, nearness = pl.pallas_call(
        functools.partial(kernel, n_cells),
        name="dislocation_step",
        out_shape=(
            pltpu.VMEM((3, SEG), F32),
            pltpu.VMEM((NB, BLK), F32),
        ),
        in_specs=[hbm] * 9,
        out_specs=(vmem, vmem),
        scratch_shapes=[
            pltpu.VMEM((3, SEG), F32),
            pltpu.VMEM((3, SEG), F32),
            pltpu.VMEM((3, SEG), F32),
            pltpu.VMEM((2, SEG), jnp.int32),
            pltpu.VMEM((2, SEG), jnp.int32),
            pltpu.VMEM((SPAN, 2, SEG), jnp.int32),
            pltpu.SMEM((NCAND,), jnp.int32),
            pltpu.SMEM((NCAND,), jnp.int32),
            pltpu.VMEM((NB, BLK), F32),
            pltpu.SMEM((NB, NENT), jnp.int32),
            pltpu.VMEM((NB, NENT), jnp.int32),
            pltpu.SMEM((NB, NENT), jnp.int32),
            pltpu.VMEM((window, 72, BLK), F32),
            pltpu.VMEM((window * NB * 49, BLK), F32),
            pltpu.VMEM((window * NB * 17, BLK), F32),
            pltpu.VMEM((NB * 25, BLK), F32),
            pltpu.VMEM((NB * 17, BLK), F32),
            pltpu.VMEM((window * NB * 33, BLK), F32),
            pltpu.VMEM((3 * NB * 33, BLK), F32),
            pltpu.VMEM((window * NB, BLK, 48), BF16),
            pltpu.VMEM((window * NB, 16, 2 * BLK), BF16),
            pltpu.VMEM((NB, 48, 2 * BLK), BF16),
            pltpu.VMEM((NB, 32, 3 * BLK), BF16),
            pltpu.VMEM((SPAN, 2, NB, BLK), jnp.int32),
            pltpu.VMEM((SPAN, 2 * SEG, BLK), BF16),
            pltpu.VMEM((SPAN, 16, 2 * SEG), F32),
            pltpu.VMEM((NB, BLK), F32),
            pltpu.VMEM((NB, BLK), F32),
            pltpu.VMEM((NB, 1, BLK), F32),
            pltpu.VMEM((SPAN, NB, 4, BLK), F32),
            pltpu.VMEM((SPAN, 3, NB, BLK), F32),
            pltpu.SemaphoreType.DMA((9,)),
            pltpu.SemaphoreType.DMA((window,)),
            pltpu.SemaphoreType.DMA((window,)),
            pltpu.SemaphoreType.DMA((SPAN,)),
            pltpu.SemaphoreType.DMA((SPAN,)),
            pltpu.SemaphoreType.DMA((5,)),
            pltpu.SemaphoreType.DMA((SPAN, 2)),
            pltpu.SemaphoreType.DMA((SPAN, 2)),
        ],
        compiler_params=pltpu.CompilerParams(
            collective_id=0, has_side_effects=True, vmem_limit_bytes=60 * 1024 * 1024
        ),
    )(
        neighbour_blocks,
        cand_target,
        cand_source,
        centres,
        seg_lines,
        burgers,
        seg_nodes,
        node_owner,
        mobility.reshape(NB, BLK),
    )
    return velocity, nearness.reshape(SEG)


def solution(mesh):
    in_specs = (
        P(None, "cells"),
        P(None, "cells"),
        P(None, "cells"),
        P("cells", "lanes"),
        P(None, "cells"),
        P(None, "cells"),
        P("cells"),
        P("cells"),
        P("cells"),
    )
    out_specs = (P(None, "cells"), P("cells"))
    return jax.shard_map(local, mesh=mesh, in_specs=in_specs, out_specs=out_specs, check_vma=False)
```
